32 devices in a mesh: group: 2 (over y), seq: 4 (over z), head: 4 (over x, core).
Axes of the slice: x: 2, y: 2, z: 4, core: 2. Of those that a mesh axis runs over, the one named last changes fastest.
Arguments:
- tokens: bfloat16 [4096, 768], P(('group', 'seq')), parts along dimension 0, may hold values from -40 to 40
- w_qkv: bfloat16 [3, 768, 768], P(None, None, 'head'), may hold values from -1 to 1
- w_out: bfloat16 [768, 768], P('head'), may hold values from -0.75 to 0.75
- gain: float32 [768], P('head'), may hold values from 0.5 to 1.5
- bias: float32 [768], P('head'), may hold values from -3 to 3
- mid_offset: int32 [12], P('head'), may hold values from 0 to 7
- far_offset: int32 [12], P('head'), may hold values from 0 to 31
Outputs:
- encoded: bfloat16 [4096, 768], P(('group', 'seq'), 'head'), parts along dimension 0
The draws below stay inside these ranges and needn't reach their ends.
There are 2 independent parts, one for each index of `group`. The reference program is written for one: setup_inputs(seed, part) draws one part's arguments, and reference() takes and returns one part's arrays. A program takes and returns all parts, laid end to end along the dimension named above; an argument that names none is the same for every part. Nothing has to cross between parts.
All inputs are finite; a program needn't handle non-finite values.
Results may differ from the reference program's by a relative error of at most 0.0085.
Values may be sent and summed in bfloat16 or wider, within the bound.
No kernel may reach another device: no remote copies, remote signals or barrier semaphores. Data moves between devices by JAX's collectives and lax.ppermute only.
A program may use at most 64 MiB of HBM per device.

```python
import math
import jax
import jax.numpy as jnp
from jax import lax

D = 768
HEADS = 12
HD = 64
TOK_DEV = 512
SEG0 = 128
R1 = 8
R2 = 32
TOKENS = 2048


def draw_tokens(key, part):
    base_key = jax.random.fold_in(key, 0)
    columns = jnp.arange(D, dtype=jnp.float32) / D
    drawn = jnp.clip(jax.random.normal(base_key, (TOKENS, D), jnp.float32), -6.0, 6.0)
    return (drawn * jnp.sqrt(3.0) ** columns).astype(jnp.bfloat16)


def draw_w_qkv(key, part):
    first = jax.random.fold_in(key, 0)
    drawn = jnp.clip(jax.random.normal(first, (3, D, D), jnp.float32), -6.0, 6.0) / jnp.sqrt(D * 1.0)
    return drawn.astype(jnp.bfloat16)


def touch_ends(values, rng, least, high):
    longest = values.shape.index(max(values.shape))
    spots = []
    for shift in (0, 1):
        where = [jax.random.randint(jax.random.fold_in(rng, axis), (), 0, length) for axis, length in enumerate(values.shape)]
        where[longest] = (where[longest] + shift) % values.shape[longest]
        spots.append(tuple(where))
    return values.at[spots[0]].set(least).at[spots[1]].set(high)


def levels(own_key, dims, cuts, low, top_value):
    factor_of, own = 1.0, jax.random.fold_in(own_key, 6)
    for axis_at, blocks in cuts:
        heights = jnp.exp(jax.random.uniform(jax.random.fold_in(own, axis_at), (blocks,), jnp.float32, low / len(cuts), top_value / len(cuts)))
        factor_of = factor_of * jnp.repeat(heights, dims[axis_at] // blocks).reshape([-1 if axis == axis_at else 1 for axis in range(len(dims))])
    return factor_of


def scatter_about(key, shape, scale, reach, cuts=(), held_as=jnp.bfloat16):
    array = scale * jax.random.normal(key, shape, jnp.float32)
    if cuts:
        array = array * levels(key, shape, cuts, -0.22, 0.18)
    return jnp.clip(array, -reach, reach).astype(held_as)


def setup_inputs(seed: int = 0, part: int = 0) -> dict:
    arg_keys = jax.random.split(jax.random.key(seed), 8)
    part_keys = jax.random.split(jax.random.fold_in(arg_keys[7], part), 8)
    return {
        "tokens": draw_tokens(jax.random.fold_in(jax.random.fold_in(arg_keys[7], part), 71), part),
        "w_qkv": draw_w_qkv(jax.random.fold_in(arg_keys[7], 71), part),
        "w_out": scatter_about(arg_keys[2], (D, D), HD ** -0.5, 0.75, ((0, 4),)),
        "gain": jnp.clip(1.0 + 0.1 * jax.random.normal(arg_keys[3], (D,), jnp.float32), 0.5, 1.5),
        "bias": scatter_about(arg_keys[4], (D,), 0.5, 3.0, ((0, 4),), jnp.float32),
        "mid_offset": touch_ends(jax.random.randint(arg_keys[5], (HEADS,), 0, R1), jax.random.fold_in(arg_keys[5], 1), 0, R1 - 1).astype(jnp.int32),
        "far_offset": touch_ends(jax.random.randint(arg_keys[6], (HEADS,), 0, R2), jax.random.fold_in(arg_keys[6], 1), 0, R2 - 1).astype(jnp.int32),
    }


epsilon = 1e-05

def attend(queries, keys_in, values_in, scale):
    scores = jnp.einsum('qhd,khd->hqk', queries.astype(jnp.float32), keys_in.astype(jnp.float32)) * scale
    peaks = lax.optimization_barrier(jnp.max(scores, axis=-1))
    shifted = jnp.exp(scores - peaks[..., None])
    masses = lax.optimization_barrier(jnp.sum(shifted, axis=-1))
    rounded = lax.optimization_barrier(shifted.astype(jnp.bfloat16))
    weights = rounded.astype(jnp.float32)
    summed = jnp.einsum('hqk,khd->qhd', weights, values_in.astype(jnp.float32))
    result = summed / jnp.transpose(masses)[:, :, None]
    log_mass = jnp.transpose(peaks + jnp.log(masses))
    return (result, log_mass)

def pick(source, offset, rate):
    folded = source.reshape(source.shape[0] // rate, rate, source.shape[1], source.shape[2])
    chosen = lax.broadcasted_iota(jnp.int32, (rate, source.shape[1]), 0) == offset[None, :]
    kept = jnp.where(chosen[None, :, :, None], folded, jnp.zeros((), source.dtype))
    return lax.optimization_barrier(jnp.sum(kept, axis=1)).astype(source.dtype)

def spread(result, log_mass, offset, rate):
    count = result.shape[0]
    chosen = lax.broadcasted_iota(jnp.int32, (rate, result.shape[1]), 0) == offset[None, :]
    full = jnp.where(chosen[None, :, :, None], result[:, None], 0.0)
    full = full.reshape(count * rate, result.shape[1], result.shape[2])
    mass_full = jnp.where(chosen[None], log_mass[:, None, :], -1e+30).reshape(count * rate, result.shape[1])
    return (full, mass_full)

def reference(tokens, w_qkv, w_out, gain, bias, mid_offset, far_offset):
    scale = 1.0 / math.sqrt(HD)
    total_rows = tokens.shape[0]
    shard_count = total_rows // TOK_DEV
    mid_length = min(8, shard_count) * TOK_DEV
    parts_list = []
    for which in range(3):
        made = jnp.dot(tokens, w_qkv[which], preferred_element_type=jnp.float32).astype(jnp.bfloat16)
        parts_list.append(made.reshape(total_rows, HEADS, HD))
    query, keyed, value = parts_list

    def run_block(triple):
        return attend(triple[0], triple[1], triple[2], scale)
    blocks = total_rows // SEG0
    near_out, near_mass = lax.map(run_block, (query.reshape(blocks, SEG0, HEADS, HD), keyed.reshape(blocks, SEG0, HEADS, HD), value.reshape(blocks, SEG0, HEADS, HD)))
    near_out = near_out.reshape(total_rows, HEADS, HD)
    near_mass = near_mass.reshape(total_rows, HEADS)
    mid_per = mid_length // R1
    mid_segs = total_rows // mid_length
    mid_query = pick(query, mid_offset, R1).reshape(mid_segs, mid_per, HEADS, HD)
    mid_keys = pick(keyed, mid_offset, R1).reshape(mid_segs, mid_per, HEADS, HD)
    mid_values = pick(value, mid_offset, R1).reshape(mid_segs, mid_per, HEADS, HD)
    mid_out, mid_mass = lax.map(run_block, (mid_query, mid_keys, mid_values))
    mid_out = mid_out.reshape(total_rows // R1, HEADS, HD)
    mid_mass = mid_mass.reshape(total_rows // R1, HEADS)
    far_query = pick(query, far_offset, R2)
    far_keys = pick(keyed, far_offset, R2)
    far_values = pick(value, far_offset, R2)
    far_block = TOK_DEV // R2

    def far_run(block_query):
        return attend(block_query, far_keys, far_values, scale)
    far_out, far_mass = lax.map(far_run, far_query.reshape(shard_count, far_block, HEADS, HD))
    far_out = far_out.reshape(total_rows // R2, HEADS, HD)
    far_mass = far_mass.reshape(total_rows // R2, HEADS)
    mid_full, mid_mfull = spread(mid_out, mid_mass, mid_offset, R1)
    far_full, far_mfull = spread(far_out, far_mass, far_offset, R2)
    top = jnp.maximum(jnp.maximum(near_mass, mid_mfull), far_mfull)
    near_weight = jnp.exp(near_mass - top)
    mid_weight = jnp.exp(mid_mfull - top)
    far_weight = jnp.exp(far_mfull - top)
    mixed = near_weight[..., None] * near_out + mid_weight[..., None] * mid_full + far_weight[..., None] * far_full
    mixed = mixed / (near_weight + mid_weight + far_weight)[..., None]
    attn = mixed.reshape(total_rows, D).astype(jnp.bfloat16)
    resid = tokens.astype(jnp.float32) + jnp.dot(attn, w_out, preferred_element_type=jnp.float32)
    mean = lax.optimization_barrier(jnp.sum(resid, axis=1)) / D
    var = lax.optimization_barrier(jnp.sum(resid * resid, axis=1)) / D - mean * mean
    normed = (resid - mean[:, None]) * lax.rsqrt(var + epsilon)[:, None] * gain + bias
    return normed.astype(jnp.bfloat16)
```

```python
from functools import partial
import math

import jax
import jax.numpy as jnp
from jax import lax
from jax.experimental import pallas as pl
from jax.experimental.pallas import tpu as pltpu
from jax.sharding import PartitionSpec as P

HEADS = 12
SEG0 = 128
R1 = 8
R2 = 32
LANES = 128
HALF = 64

epsilon = 1e-05
f32 = jnp.float32
bf16 = jnp.bfloat16

NT = (((1,), (1,)), ((), ()))


def lane_half(shape):
    return lax.broadcasted_iota(jnp.int32, shape, 1) < HALF


def acc_low(head):
    return head % 2 == 0


def project_kernel(mo, fo, x_ref, w_ref, qkv_ref, kvp_ref, qp_ref, scr):
    rows = x_ref.shape[0]
    mid, far = rows // R1, rows // R2
    per = mid + far
    q = [w_ref[0, h * HALF : (h + 1) * HALF] for h in range(3)]
    k = [w_ref[1, h * HALF : (h + 1) * HALF] for h in range(3)]
    v = [w_ref[2, h * HALF : (h + 1) * HALF] for h in range(3)]
    w = jnp.concatenate(
        [v[0], k[0], k[1], v[1], v[2], k[2], q[1], q[0], q[2], q[2]], axis=0
    )
    y = lax.dot_general(x_ref[...], w, NT, preferred_element_type=f32).astype(bf16)
    qkv_ref[...] = y
    for i in range(5):
        scr[i] = y[:, i * LANES : (i + 1) * LANES].astype(f32)
    for h in range(3):
        asked = 3 + h // 2
        low = lane_half((mid, LANES))
        keep = jnp.logical_not(low) if acc_low(h) else low
        mid_rows = pl.ds(mo[h], mid, stride=R1)
        far_rows = pl.ds(fo[h], far, stride=R2)
        kvp_ref[h * per : h * per + mid] = scr[h, mid_rows].astype(bf16)
        kvp_ref[h * per + mid : (h + 1) * per] = scr[h, far_rows].astype(bf16)
        qp_ref[h * per : h * per + mid] = jnp.where(keep, scr[asked, mid_rows], 0.0).astype(bf16)
        qp_ref[h * per + mid : (h + 1) * per] = jnp.where(
            keep[:far], scr[asked, far_rows], 0.0
        ).astype(bf16)


def soft(queries, keys_values, head, factor):
    s = lax.dot_general(queries, keys_values, NT, preferred_element_type=f32)
    peak = jnp.max(s, axis=1, keepdims=True)
    p = jnp.exp2((s - peak) * factor).astype(bf16)
    low = lane_half(keys_values.shape)
    is_value = low if acc_low(head) else jnp.logical_not(low)
    values = jnp.where(is_value, keys_values, jnp.ones((), bf16))
    return peak, jnp.dot(p, values, preferred_element_type=f32)


def near_kernel(factor, mo, fo, qkv_ref, near_ref, am_ref, pk_ref, am_scr, pk_scr):
    rows = qkv_ref.shape[0]
    mid, far = rows // R1, rows // R2
    per = mid + far
    low = lane_half((SEG0, LANES))
    for b in range(rows // SEG0):
        at = slice(b * SEG0, (b + 1) * SEG0)
        done = []
        for h in range(3):
            keep = jnp.logical_not(low) if acc_low(h) else low
            first = (3 + h // 2) * LANES
            queries = jnp.where(keep, qkv_ref[at, first : first + LANES], jnp.zeros((), bf16))
            peak, am = soft(queries, qkv_ref[at, h * LANES : (h + 1) * LANES], h, factor)
            am_scr[h, at] = am
            pk_scr[h, at] = jnp.broadcast_to(peak, am.shape)
            done.append(am / pltpu.roll(am, HALF, 1))
        near_ref[at, :LANES] = jnp.where(low, done[0], done[1]).astype(bf16)
        near_ref[at, LANES:] = jnp.where(low, done[2], 0.0).astype(bf16)
    for h in range(3):
        for first, picked in (
            (h * per, pl.ds(mo[h], mid, stride=R1)),
            (h * per + mid, pl.ds(fo[h], far, stride=R2)),
        ):
            count = mid if first == h * per else far
            am_ref[first : first + count] = am_scr[h, picked]
            pk_ref[first : first + count] = pk_scr[h, picked]


def merge_kernel(factor, mid_n, far_n, mo, fo, qp_ref, am_ref, pk_ref, *rest):
    mids, fars = rest[:mid_n], rest[mid_n : mid_n + far_n]
    corr_ref, am_scr, pk_scr = rest[mid_n + far_n :]
    mid, far = corr_ref.shape[0] * 4 // 5, corr_ref.shape[0] // 5
    per = mid + far
    out_mid, out_far = [], []
    for h in range(3):
        own = slice(h * per, h * per + mid)
        own_far = slice(h * per + mid, (h + 1) * per)
        kv_mid = jnp.concatenate([m[h] for m in mids], axis=0)
        kv_far = jnp.concatenate([m[h] for m in fars], axis=0)
        peak_mid, am_mid = soft(qp_ref[own], kv_mid, h, factor)
        peak_far, am_far = soft(qp_ref[own_far], kv_far, h, factor)
        peak_mid = jnp.broadcast_to(peak_mid, am_mid.shape)
        am_scr[h] = am_mid
        pk_scr[h] = peak_mid
        near_peak, near_am = pk_ref[own], am_ref[own]
        top = jnp.maximum(near_peak, peak_mid)
        total = (
            jnp.exp2((near_peak - top) * factor) * near_am
            + jnp.exp2((peak_mid - top) * factor) * am_mid
        )
        out_mid.append(total / pltpu.roll(total, HALF, 1))
        shared = pl.ds(fo[h] // R1, far, stride=R2 // R1)
        also = fo[h] % R1 == mo[h]
        both_peak = jnp.where(also, pk_scr[h, shared], -1e30)
        both_am = am_scr[h, shared]
        near_peak, near_am = pk_ref[own_far], am_ref[own_far]
        top = jnp.maximum(jnp.maximum(near_peak, both_peak), peak_far)
        total = (
            jnp.exp2((near_peak - top) * factor) * near_am
            + jnp.exp2((both_peak - top) * factor) * both_am
            + jnp.exp2((peak_far - top) * factor) * am_far
        )
        out_far.append(total / pltpu.roll(total, HALF, 1))
    for first, out in ((0, out_mid), (mid, out_far)):
        at = slice(first, first + out[0].shape[0])
        low = lane_half(out[0].shape)
        corr_ref[at, :LANES] = jnp.where(low, out[0], out[1]).astype(bf16)
        corr_ref[at, LANES:] = jnp.where(low, out[2], 0.0).astype(bf16)


def output_kernel(head_count, place, mo, fo, x_ref, gain_ref, bias_ref, *rest):
    near, corr, weights = (rest[i * head_count : (i + 1) * head_count] for i in range(3))
    out_ref, attn_scr, resid_scr = rest[3 * head_count :]
    rows, width = x_ref.shape
    mid, far = rows // R1, rows // R2
    cols = width // head_count
    resid = x_ref[...].astype(f32)
    low = lane_half((rows, LANES))
    for r in range(head_count):
        for h in range(3):
            tile = slice(h // 2 * LANES, (h // 2 + 1) * LANES)
            attn_scr[r, h] = near[r][:, tile].astype(f32)
            attn_scr[r, h, pl.ds(mo[r, h], mid, stride=R1)] = corr[r][:mid, tile].astype(f32)
            attn_scr[r, h, pl.ds(fo[r, h], far, stride=R2)] = corr[r][mid:, tile].astype(f32)
        pair = jnp.where(low, attn_scr[r, 0], attn_scr[r, 1]).astype(bf16)
        attn = jnp.concatenate([pair, attn_scr[r, 2].astype(bf16)[:, :HALF]], axis=1)
        resid += jnp.dot(attn, weights[r][...], preferred_element_type=f32)
    mean = jnp.sum(resid, axis=1, keepdims=True) / width
    var = jnp.sum(resid * resid, axis=1, keepdims=True) / width - mean * mean
    inv = lax.rsqrt(var + epsilon)
    resid_scr[...] = resid
    for i in range(head_count):

        @pl.when(place[0] == i)
        def _():
            mine = resid_scr[:, i * cols : (i + 1) * cols]
            normed = (mine - mean) * inv * gain_ref[...] + bias_ref[...]
            out_ref[...] = normed.T.astype(bf16)


def vmem(*shape_dtypes):
    return [pltpu.VMEM(shape, dtype) for shape, dtype in shape_dtypes]


IN_VMEM = pl.BlockSpec(memory_space=pltpu.VMEM)
IN_SMEM = pl.BlockSpec(memory_space=pltpu.SMEM)


def call(kernel, outs, scratch, scalars, arrays, name):
    return pl.pallas_call(
        kernel,
        out_shape=outs,
        in_specs=[IN_SMEM] * len(scalars) + [IN_VMEM] * len(arrays),
        out_specs=jax.tree.map(lambda _: IN_VMEM, outs),
        scratch_shapes=vmem(*scratch),
        compiler_params=pltpu.CompilerParams(vmem_limit_bytes=48 << 20),
        name=name,
    )(*scalars, *arrays)


def local(tokens, w_qkv, w_out, gain, bias, mid_offset, far_offset):
    rows, width = tokens.shape
    heads_here = mid_offset.shape[0]
    head_size = width // HEADS
    cols = heads_here * head_size
    factor = math.log2(math.e) / math.sqrt(head_size)
    mid, far = rows // R1, rows // R2
    per = mid + far
    shape = jax.ShapeDtypeStruct

    qkv, kvp, qp = call(
        project_kernel,
        (
            shape((rows, 5 * LANES), bf16),
            shape((3 * per, LANES), bf16),
            shape((3 * per, LANES), bf16),
        ),
        [((5, rows, LANES), f32)],
        (mid_offset, far_offset),
        (tokens, jnp.swapaxes(w_qkv, 1, 2)),
        "project",
    )

    seq_count = lax.axis_size("seq")
    mid_devs = min(8, seq_count)

    def within(step):
        return [
            (i, i // mid_devs * mid_devs + (i + step) % mid_devs) for i in range(seq_count)
        ]

    if mid_devs == seq_count:
        pieces = [kvp] + [lax.ppermute(kvp, "seq", within(s)) for s in range(1, mid_devs)]
        pieces = [p.reshape(3, per, LANES) for p in pieces]
        mids = [p[:, :mid] for p in pieces]
        fars = [p[:, mid:] for p in pieces]
    else:
        split = kvp.reshape(3, per, LANES)
        piece = split[:, :mid]
        mids = [piece] + [lax.ppermute(piece, "seq", within(s)) for s in range(1, mid_devs)]
        fars = [lax.all_gather(split[:, mid:], "seq", axis=1, tiled=True)]

    head_count = lax.axis_size("head")
    if head_count & (head_count - 1) == 0:
        paths = [[(i, i ^ r) for i in range(head_count)] for r in range(head_count)]
    else:
        paths = [[(i, (i + r) % head_count) for i in range(head_count)] for r in range(head_count)]

    def spread(array):
        return [array] + [lax.ppermute(array, "head", paths[r]) for r in range(1, head_count)]

    def relay(array):
        if head_count != 4:
            return spread(array)
        across = lax.ppermute(array, "head", paths[2])
        beside = lax.ppermute(array, "head", paths[1])
        return [array, beside, across, lax.ppermute(across, "head", paths[1])]

    weights = relay(w_out)
    offsets = spread(jnp.concatenate([mid_offset, far_offset]))
    offsets = jnp.stack(offsets)

    near, am, pk = call(
        partial(near_kernel, factor),
        (
            shape((rows, 2 * LANES), bf16),
            shape((3 * per, LANES), f32),
            shape((3 * per, LANES), f32),
        ),
        [((3, rows, LANES), f32)] * 2,
        (mid_offset, far_offset),
        (qkv,),
        "near",
    )
    nears = relay(near)

    corr = call(
        partial(merge_kernel, factor, len(mids), len(fars)),
        shape((per, 2 * LANES), bf16),
        [((3, mid, LANES), f32)] * 2,
        (mid_offset, far_offset),
        (qp, am, pk, *mids, *fars),
        "merge",
    )
    corrs = spread(corr)

    out = call(
        partial(output_kernel, head_count),
        shape((cols, rows), bf16),
        [((head_count, 3, rows, LANES), f32), ((rows, width), f32)],
        (
            lax.axis_index("head").reshape(1),
            offsets[:, :heads_here],
            offsets[:, heads_here:],
        ),
        (tokens, gain.reshape(1, cols), bias.reshape(1, cols), *nears, *corrs, *weights),
        "output",
    )
    return out.T


def solution(mesh):
    in_specs = (
        P(("group", "seq"), None),
        P(None, None, "head"),
        P("head", None),
        P("head"),
        P("head"),
        P("head"),
        P("head"),
    )
    out_specs = P(("group", "seq"), "head")
    return jax.shard_map(local, mesh=mesh, in_specs=in_specs, out_specs=out_specs, check_vma=False)
```

```python
from functools import partial
import math

import jax
import jax.numpy as jnp
from jax import lax
from jax.experimental import pallas as pl
from jax.experimental.pallas import tpu as pltpu
from jax.sharding import PartitionSpec as P

HEADS = 12
SEG0 = 128
R1 = 8
R2 = 32
LANES = 128
HALF = 64

epsilon = 1e-05
f32 = jnp.float32
bf16 = jnp.bfloat16

NT = (((1,), (1,)), ((), ()))


def lane_half(shape):
    return lax.broadcasted_iota(jnp.int32, shape, 1) < HALF


def acc_low(head):
    return head % 2 == 0


def project_kernel(mo, fo, x_hbm, w_hbm, qkv_ref, kvp_ref, qp_ref, x_ref, w_ref, scr, x_sem, w_sem):
    rows = x_ref.shape[0]
    mid, far = rows // R1, rows // R2
    per = mid + far
    pieces, piece = x_sem.shape[0], rows // x_sem.shape[0]
    w_pieces, w_piece = w_sem.shape[1], w_ref.shape[1] // w_sem.shape[1]

    def w_copy(i, j):
        at = pl.ds(j * w_piece, w_piece)
        return pltpu.make_async_copy(w_hbm.at[i, at], w_ref.at[i, at], w_sem.at[i, j])

    def x_copy(i):
        at = pl.ds(i * piece, piece)
        return pltpu.make_async_copy(x_hbm.at[at], x_ref.at[at], x_sem.at[i])

    copies = [w_copy(i, j) for i in range(3) for j in range(w_pieces)]
    copies += [x_copy(i) for i in range(pieces)]
    for copy in copies:
        copy.start()
    for copy in copies:
        copy.wait()
    q = [w_ref[0, h * HALF : (h + 1) * HALF] for h in range(3)]
    k = [w_ref[1, h * HALF : (h + 1) * HALF] for h in range(3)]
    v = [w_ref[2, h * HALF : (h + 1) * HALF] for h in range(3)]
    w = jnp.concatenate([v[0], k[0], k[1], v[1], v[2], k[2], q[1], q[0], q[2], q[2]], axis=0)
    step = rows // 2
    for first in range(0, rows, step):
        at = slice(first, first + step)
        y = lax.dot_general(x_ref[at], w, NT, preferred_element_type=f32).astype(bf16)
        qkv_ref[at] = y
        for i in range(5):
            scr[i, at] = y[:, i * LANES : (i + 1) * LANES].astype(f32)
    for h in range(3):
        asked = 3 + h // 2
        low = lane_half((mid, LANES))
        keep = jnp.logical_not(low) if acc_low(h) else low
        mid_rows = pl.ds(mo[h], mid, stride=R1)
        far_rows = pl.ds(fo[h], far, stride=R2)
        kvp_ref[h * per : h * per + mid] = scr[h, mid_rows].astype(bf16)
        kvp_ref[h * per + mid : (h + 1) * per] = scr[h, far_rows].astype(bf16)
        qp_ref[h * per : h * per + mid] = jnp.where(keep, scr[asked, mid_rows], 0.0).astype(bf16)
        qp_ref[h * per + mid : (h + 1) * per] = jnp.where(
            keep[:far], scr[asked, far_rows], 0.0
        ).astype(bf16)


def scores(queries, keys_values):
    return lax.dot_general(queries, keys_values, NT, preferred_element_type=f32)


def soften(s, factor):
    peak = jnp.max(s, axis=1, keepdims=True)
    return peak, jnp.exp2((s - peak) * factor).astype(bf16)


def weigh(p, keys_values, head):
    low = lane_half(keys_values.shape)
    is_value = low if acc_low(head) else jnp.logical_not(low)
    values = jnp.where(is_value, keys_values, jnp.ones((), bf16))
    return jnp.dot(p, values, preferred_element_type=f32)


def swap(x):
    return pltpu.roll(x, HALF, 1)


def pair(a, b):
    low = lane_half(a.shape)
    return (jnp.where(low, a, b) / swap(jnp.where(low, b, a))).astype(bf16)


def fold(x):
    half = x.shape[0] // 2
    a, b = x[:half], x[half:]
    low = lane_half(a.shape)
    return (jnp.where(low, a, swap(b)) / jnp.where(low, swap(a), b)).astype(bf16)


def near_kernel(factor, mo, fo, qkv_ref, near_ref, am_ref, pk_ref, am_scr, pk_scr):
    rows = qkv_ref.shape[0]
    mid, far = rows // R1, rows // R2
    per = mid + far
    low = lane_half((SEG0, LANES))
    blocks = rows // SEG0
    units = [(b, h) for b in range(blocks) for h in range(3)]

    def rows_of(b):
        return slice(b * SEG0, (b + 1) * SEG0)

    def kv(b, h):
        return qkv_ref[rows_of(b), h * LANES : (h + 1) * LANES]

    def ask(b, h):
        keep = jnp.logical_not(low) if acc_low(h) else low
        first = (3 + h // 2) * LANES
        q = qkv_ref[rows_of(b), first : first + LANES]
        return scores(jnp.where(keep, q, jnp.zeros((), bf16)), kv(b, h))

    s = {u: ask(*u) for u in units[:3]}
    am = {}
    for i, u in enumerate(units):
        if i + 3 < len(units):
            s[units[i + 3]] = ask(*units[i + 3])
        b, h = u
        peak, p = soften(s.pop(u), factor)
        am[u] = weigh(p, kv(b, h), h)
        am_scr[h, rows_of(b)] = am[u]
        pk_scr[h, rows_of(b)] = jnp.broadcast_to(peak, am[u].shape)
        if h == 2:
            near_ref[rows_of(b)] = pair(am.pop((b, 0)), am.pop((b, 1)))
    near_ref[rows : rows + rows // 2] = fold(am_scr[2])
    lane = lax.broadcasted_iota(jnp.int32, (16, LANES), 1)
    told = jnp.zeros((16, LANES), jnp.int32)
    for h in range(3):
        told = jnp.where(lane == h, mo[h], jnp.where(lane == 3 + h, fo[h], told))
    near_ref[rows + rows // 2 :] = told.astype(f32).astype(bf16)
    for h in range(3):
        own, own_far = slice(h * per, h * per + mid), slice(h * per + mid, (h + 1) * per)
        mid_rows = pl.ds(mo[h], mid, stride=R1)
        far_rows = pl.ds(fo[h], far, stride=R2)
        am_ref[own], am_ref[own_far] = am_scr[h, mid_rows], am_scr[h, far_rows]
        pk_ref[own], pk_ref[own_far] = pk_scr[h, mid_rows], pk_scr[h, far_rows]


def merge_kernel(factor, mid_n, far_n, mo, fo, qp_ref, am_ref, pk_ref, *rest):
    mids, fars = rest[:mid_n], rest[mid_n : mid_n + far_n]
    corr_ref, am_scr, pk_scr = rest[mid_n + far_n :]
    per = qp_ref.shape[0] // 3
    far = per * R1 // (R1 + R2)
    mid = per - far
    heads = range(3)
    own = [slice(h * per, h * per + mid) for h in heads]
    own_far = [slice(h * per + mid, (h + 1) * per) for h in heads]

    def joined(refs, h, whole, at):
        return jnp.concatenate([m[at[h]] if m.shape[0] == 3 * per else m[h] for m in refs], axis=0)

    kv_mid = [joined(mids, h, per, own) for h in heads]
    kv_far = [joined(fars, h, per, own_far) for h in heads]
    s_mid = [scores(qp_ref[own[h]], kv_mid[h]) for h in heads]
    s_far = [scores(qp_ref[own_far[h]], kv_far[h]) for h in heads]
    soft_mid = [soften(s, factor) for s in s_mid]
    soft_far = [soften(s, factor) for s in s_far]
    am_mid = [weigh(soft_mid[h][1], kv_mid[h], h) for h in heads]
    am_far = [weigh(soft_far[h][1], kv_far[h], h) for h in heads]
    out_mid, out_far = [], []
    for h in heads:
        peak_mid = jnp.broadcast_to(soft_mid[h][0], am_mid[h].shape)
        am_scr[h] = am_mid[h]
        pk_scr[h] = peak_mid
        near_peak, near_am = pk_ref[own[h]], am_ref[own[h]]
        top = jnp.maximum(near_peak, peak_mid)
        out_mid.append(
            jnp.exp2((near_peak - top) * factor) * near_am
            + jnp.exp2((peak_mid - top) * factor) * am_mid[h]
        )
    for h in heads:
        shared = pl.ds(fo[h] // R1, far, stride=R2 // R1)
        also = fo[h] % R1 == mo[h]
        both_peak = jnp.where(also, pk_scr[h, shared], -1e30)
        both_am = am_scr[h, shared]
        near_peak, near_am = pk_ref[own_far[h]], am_ref[own_far[h]]
        top = jnp.maximum(jnp.maximum(near_peak, both_peak), soft_far[h][0])
        out_far.append(
            jnp.exp2((near_peak - top) * factor) * near_am
            + jnp.exp2((both_peak - top) * factor) * both_am
            + jnp.exp2((soft_far[h][0] - top) * factor) * am_far[h]
        )
    corr_ref[:mid] = pair(out_mid[0], out_mid[1])
    corr_ref[mid:per] = pair(out_far[0], out_far[1])
    corr_ref[per : per + mid // 2] = fold(out_mid[2])
    corr_ref[per + mid // 2 :] = fold(out_far[2])


def output_kernel(head_count, place, mo, fo, x_ref, gain_ref, bias_ref, *rest):
    near, corr, weights = (rest[i * head_count : (i + 1) * head_count] for i in range(3))
    out_ref, attn_scr, resid_scr = rest[3 * head_count :]
    rows, width = x_ref.shape
    mid, far = rows // R1, rows // R2
    half = rows // 2
    per = mid + far
    cols = width // head_count
    for r in range(head_count):
        attn_scr[r] = near[r][:rows].astype(f32)
    low = lane_half((half, LANES))
    for r in range(0, head_count, 2):
        even = near[r][rows : rows + half].astype(f32)
        odd = near[r + 1][rows : rows + half].astype(f32)
        attn_scr[head_count + r // 2, :half] = jnp.where(low, even, swap(odd))
        attn_scr[head_count + r // 2, half:] = jnp.where(low, swap(even), odd)

    def patch(tile, to_low, first, count, stride, value):
        at = pl.ds(first, count, stride=stride)
        low = lane_half(value.shape)
        keep = low if to_low else jnp.logical_not(low)
        attn_scr[tile, at] = jnp.where(keep, value, attn_scr[tile, at])

    for offset, stride, count, first, folded in (
        (mo, R1, mid, 0, per),
        (fo, R2, far, mid, per + mid // 2),
    ):
        for r in range(head_count):
            both = corr[r][first : first + count].astype(f32)
            patch(r, True, offset[r, 0], count, stride, both)
            patch(r, False, offset[r, 1], count, stride, both)
            third = corr[r][folded : folded + count // 2].astype(f32)
            turned = swap(third)
            tile, to_low = head_count + r // 2, r % 2 == 0
            upper, lower = (third, turned) if to_low else (turned, third)
            patch(tile, to_low, offset[r, 2], count // 2, stride, upper)
            patch(tile, to_low, offset[r, 2] + half, count // 2, stride, lower)

    w = jnp.concatenate(
        [weights[r][:LANES] for r in range(head_count)]
        + [weights[r][LANES:] for r in range(head_count)],
        axis=0,
    )
    for first in (0, half):
        at = slice(first, first + half)
        attn = jnp.concatenate(
            [attn_scr[t, at].astype(bf16) for t in range(attn_scr.shape[0])], axis=1
        )
        resid = x_ref[at].astype(f32) + jnp.dot(attn, w, preferred_element_type=f32)
        mean = jnp.sum(resid, axis=1, keepdims=True) / width
        var = jnp.sum(resid * resid, axis=1, keepdims=True) / width - mean * mean
        resid_scr[at] = (resid - mean) * lax.rsqrt(var + epsilon)
    for i in range(head_count):

        @pl.when(place[0] == i)
        def _():
            mine = resid_scr[:, i * cols : (i + 1) * cols]
            out_ref[...] = (mine * gain_ref[...] + bias_ref[...]).T.astype(bf16)


IN_VMEM = pl.BlockSpec(memory_space=pltpu.VMEM)
IN_SMEM = pl.BlockSpec(memory_space=pltpu.SMEM)
IN_HBM = pl.BlockSpec(memory_space=pltpu.HBM)


def call(kernel, outs, scratch, scalars, arrays, name, cost, held=IN_VMEM):
    return pl.pallas_call(
        kernel,
        out_shape=outs,
        in_specs=[IN_SMEM] * len(scalars) + [held] * len(arrays),
        out_specs=jax.tree.map(lambda _: IN_VMEM, outs),
        scratch_shapes=scratch,
        compiler_params=pltpu.CompilerParams(vmem_limit_bytes=32 << 20),
        name=name,
        cost_estimate=pl.CostEstimate(flops=cost, transcendentals=0, bytes_accessed=4 << 20),
    )(*scalars, *arrays)


def local(tokens, w_qkv, w_out, gain, bias, mid_offset, far_offset):
    rows, width = tokens.shape
    heads_here = mid_offset.shape[0]
    head_size = width // HEADS
    cols = heads_here * head_size
    factor = math.log2(math.e) / math.sqrt(head_size)
    mid, far = rows // R1, rows // R2
    per = mid + far
    shape = jax.ShapeDtypeStruct
    after = lax.optimization_barrier

    head_count = lax.axis_size("head")
    if head_count & (head_count - 1) == 0:
        paths = [[(i, i ^ r) for i in range(head_count)] for r in range(head_count)]
    else:
        paths = [[(i, (i + r) % head_count) for i in range(head_count)] for r in range(head_count)]

    def to(array, r):
        return lax.ppermute(array, "head", paths[r])

    def spread(array):
        return [array] + [to(array, r) for r in range(1, head_count)]

    two_step = head_count == 4

    qkv, kvp, qp = call(
        project_kernel,
        (
            shape((rows, 5 * LANES), bf16),
            shape((3 * per, LANES), bf16),
            shape((3 * per, LANES), bf16),
        ),
        [
            pltpu.VMEM((rows, width), bf16),
            pltpu.VMEM((3, cols, width), bf16),
            pltpu.VMEM((5, rows, LANES), f32),
            pltpu.SemaphoreType.DMA((4,)),
            pltpu.SemaphoreType.DMA((3, 2)),
        ],
        (mid_offset, far_offset),
        (tokens, jnp.swapaxes(w_qkv, 1, 2)),
        "project",
        2 * rows * width * 3 * cols,
        IN_HBM,
    )

    seq_count = lax.axis_size("seq")
    mid_devs = min(8, seq_count)

    def within(step):
        return [
            (i, i // mid_devs * mid_devs + (i + step) % mid_devs) for i in range(seq_count)
        ]

    if mid_devs == seq_count:
        mids = [kvp] + [lax.ppermute(kvp, "seq", within(s)) for s in range(1, mid_devs)]
        fars = None
    else:
        split = kvp.reshape(3, per, LANES)
        piece = split[:, :mid]
        mids = [piece] + [lax.ppermute(piece, "seq", within(s)) for s in range(1, mid_devs)]
        fars = [lax.all_gather(split[:, mid:], "seq", axis=1, tiled=True)]

    if two_step:
        across = to(w_out, 2)
        beside = to(after((w_out, kvp))[0], 1)
        qkv, beside = after((qkv, beside))
    else:
        weights = spread(w_out)

    near, am, pk = call(
        partial(near_kernel, factor),
        (
            shape((rows + rows // 2 + 16, LANES), bf16),
            shape((3 * per, LANES), f32),
            shape((3 * per, LANES), f32),
        ),
        [pltpu.VMEM((3, rows, LANES), f32)] * 2,
        (mid_offset, far_offset),
        (qkv,),
        "near",
        1 << 28,
    )
    if two_step:
        last = to(after((across, beside))[0], 1)
        weights = [w_out, beside, across, last]
        near_across = to(after((near, across))[0], 2)
        near_beside = to(after((near, last))[0], 1)
        near_last = to(after((near_across, near_beside))[0], 1)
        nears = [near, near_beside, near_across, near_last]
    else:
        nears = spread(near)

    corr = call(
        partial(merge_kernel, factor, len(mids), len(fars or mids)),
        shape((per + per // 2, LANES), bf16),
        [pltpu.VMEM((3, mid, LANES), f32)] * 2,
        (mid_offset, far_offset),
        (qp, am, pk, *mids, *(fars or mids)),
        "merge",
        1 << 27,
    )
    corrs = spread(corr)
    told = [n[rows + rows // 2, : 2 * heads_here].astype(jnp.int32) for n in nears]
    told = jnp.stack(told)

    out = call(
        partial(output_kernel, head_count),
        shape((cols, rows), bf16),
        [
            pltpu.VMEM((head_count + head_count // 2, rows, LANES), f32),
            pltpu.VMEM((rows, width), f32),
        ],
        (lax.axis_index("head").reshape(1), told[:, :heads_here], told[:, heads_here:]),
        (tokens, gain.reshape(1, cols), bias.reshape(1, cols), *nears, *corrs, *weights),
        "output",
        2 * rows * width * width,
    )
    return out.T


def solution(mesh):
    in_specs = (
        P(("group", "seq"), None),
        P(None, None, "head"),
        P("head", None),
        P("head"),
        P("head"),
        P("head"),
        P("head"),
    )
    out_specs = P(("group", "seq"), "head")
    return jax.shard_map(local, mesh=mesh, in_specs=in_specs, out_specs=out_specs, check_vma=False)
```

```python
from functools import partial
import math

import jax
import jax.numpy as jnp
from jax import lax
from jax.experimental import pallas as pl
from jax.experimental.pallas import tpu as pltpu
from jax.sharding import PartitionSpec as P

HEADS = 12
SEG0 = 128
R1 = 8
R2 = 32
LANES = 128
HALF = 64

epsilon = 1e-05
f32 = jnp.float32
bf16 = jnp.bfloat16

NT = (((1,), (1,)), ((), ()))


def lane_half(shape):
    return lax.broadcasted_iota(jnp.int32, shape, 1) < HALF


def acc_low(head):
    return head % 2 == 0


def project_kernel(mo, fo, x_hbm, w_hbm, qkv_ref, kvp_ref, qp_ref, x_ref, w_ref, scr, x_sem, w_sem):
    rows = x_ref.shape[0]
    mid, far = rows // R1, rows // R2
    per = mid + far
    pieces, piece = x_sem.shape[0], rows // x_sem.shape[0]
    w_pieces, w_piece = w_sem.shape[1], w_ref.shape[1] // w_sem.shape[1]

    def w_copy(i, j):
        at = pl.ds(j * w_piece, w_piece)
        return pltpu.make_async_copy(w_hbm.at[i, at], w_ref.at[i, at], w_sem.at[i, j])

    def x_copy(i):
        at = pl.ds(i * piece, piece)
        return pltpu.make_async_copy(x_hbm.at[at], x_ref.at[at], x_sem.at[i])

    copies = [w_copy(i, j) for i in range(3) for j in range(w_pieces)]
    copies += [x_copy(i) for i in range(pieces)]
    for copy in copies:
        copy.start()
    for copy in copies:
        copy.wait()
    q = [w_ref[0, h * HALF : (h + 1) * HALF] for h in range(3)]
    k = [w_ref[1, h * HALF : (h + 1) * HALF] for h in range(3)]
    v = [w_ref[2, h * HALF : (h + 1) * HALF] for h in range(3)]
    w = jnp.concatenate([v[0], k[0], k[1], v[1], v[2], k[2], q[1], q[0], q[2], q[2]], axis=0)
    step = rows // 2
    for first in range(0, rows, step):
        at = slice(first, first + step)
        y = lax.dot_general(x_ref[at], w, NT, preferred_element_type=f32).astype(bf16)
        qkv_ref[at] = y
        for i in range(5):
            scr[i, at] = y[:, i * LANES : (i + 1) * LANES].astype(f32)
    for h in range(3):
        asked = 3 + h // 2
        low = lane_half((mid, LANES))
        keep = jnp.logical_not(low) if acc_low(h) else low
        mid_rows = pl.ds(mo[h], mid, stride=R1)
        far_rows = pl.ds(fo[h], far, stride=R2)
        kvp_ref[h * per : h * per + mid] = scr[h, mid_rows].astype(bf16)
        kvp_ref[h * per + mid : (h + 1) * per] = scr[h, far_rows].astype(bf16)
        qp_ref[h * per : h * per + mid] = jnp.where(keep, scr[asked, mid_rows], 0.0).astype(bf16)
        qp_ref[h * per + mid : (h + 1) * per] = jnp.where(
            keep[:far], scr[asked, far_rows], 0.0
        ).astype(bf16)


def scores(queries, keys_values):
    return lax.dot_general(queries, keys_values, NT, preferred_element_type=f32)


def soften(s, factor):
    peak = jnp.max(s, axis=1, keepdims=True)
    return peak, jnp.exp2((s - peak) * factor).astype(bf16)


def weigh(p, keys_values, head):
    low = lane_half(keys_values.shape)
    is_value = low if acc_low(head) else jnp.logical_not(low)
    values = jnp.where(is_value, keys_values, jnp.ones((), bf16))
    return jnp.dot(p, values, preferred_element_type=f32)


def swap(x):
    return pltpu.roll(x, HALF, 1)


def pair(a, b):
    low = lane_half(a.shape)
    return jnp.where(low, a, b) / swap(jnp.where(low, b, a))


def fold(x):
    half = x.shape[0] // 2
    a, b = x[:half], x[half:]
    low = lane_half(a.shape)
    return jnp.where(low, a, swap(b)) / jnp.where(low, swap(a), b)


def near_kernel(
    factor, mo, fo, qkv_ref, gain_ref, bias_ref, near_ref, am_ref, pk_ref, gb_ref, am_scr, pk_scr
):
    gb_ref[0:1] = gain_ref[...]
    gb_ref[1:2] = bias_ref[...]
    rows = qkv_ref.shape[0]
    mid, far = rows // R1, rows // R2
    per = mid + far
    low = lane_half((SEG0, LANES))
    blocks = rows // SEG0
    units = [(b, h) for b in range(blocks) for h in range(3)]

    def rows_of(b):
        return slice(b * SEG0, (b + 1) * SEG0)

    def kv(b, h):
        return qkv_ref[rows_of(b), h * LANES : (h + 1) * LANES]

    def ask(b, h):
        keep = jnp.logical_not(low) if acc_low(h) else low
        first = (3 + h // 2) * LANES
        q = qkv_ref[rows_of(b), first : first + LANES]
        return scores(jnp.where(keep, q, jnp.zeros((), bf16)), kv(b, h))

    s = {u: ask(*u) for u in units[:3]}
    am = {}
    for i, u in enumerate(units):
        if i + 3 < len(units):
            s[units[i + 3]] = ask(*units[i + 3])
        b, h = u
        peak, p = soften(s.pop(u), factor)
        am[u] = weigh(p, kv(b, h), h)
        am_scr[h, rows_of(b)] = am[u]
        pk_scr[h, rows_of(b)] = jnp.broadcast_to(peak, am[u].shape)
        if h == 2:
            near_ref[rows_of(b)] = pair(am.pop((b, 0)), am.pop((b, 1)))
    near_ref[rows:] = fold(am_scr[2])
    for h in range(3):
        own, own_far = slice(h * per, h * per + mid), slice(h * per + mid, (h + 1) * per)
        mid_rows = pl.ds(mo[h], mid, stride=R1)
        far_rows = pl.ds(fo[h], far, stride=R2)
        am_ref[own], am_ref[own_far] = am_scr[h, mid_rows], am_scr[h, far_rows]
        pk_ref[own], pk_ref[own_far] = pk_scr[h, mid_rows], pk_scr[h, far_rows]


def merge_kernel(factor, mid_n, far_n, mo, fo, near_ref, qp_ref, am_ref, pk_ref, *rest):
    mids, fars = rest[:mid_n], rest[mid_n : mid_n + far_n]
    attn_ref, attn_scr, am_scr, pk_scr = rest[mid_n + far_n :]
    rows = near_ref.shape[0] * 2 // 3
    attn_scr[...] = near_ref[...]
    per = qp_ref.shape[0] // 3
    far = per * R1 // (R1 + R2)
    mid = per - far
    heads = range(3)
    own = [slice(h * per, h * per + mid) for h in heads]
    own_far = [slice(h * per + mid, (h + 1) * per) for h in heads]

    def joined(refs, h, whole, at):
        return jnp.concatenate([m[at[h]] if m.shape[0] == 3 * per else m[h] for m in refs], axis=0)

    kv_mid = [joined(mids, h, per, own) for h in heads]
    kv_far = [joined(fars, h, per, own_far) for h in heads]
    s_mid = [scores(qp_ref[own[h]], kv_mid[h]) for h in heads]
    s_far = [scores(qp_ref[own_far[h]], kv_far[h]) for h in heads]
    soft_mid = [soften(s, factor) for s in s_mid]
    soft_far = [soften(s, factor) for s in s_far]
    am_mid = [weigh(soft_mid[h][1], kv_mid[h], h) for h in heads]
    am_far = [weigh(soft_far[h][1], kv_far[h], h) for h in heads]
    out_mid, out_far = [], []
    for h in heads:
        peak_mid = jnp.broadcast_to(soft_mid[h][0], am_mid[h].shape)
        am_scr[h] = am_mid[h]
        pk_scr[h] = peak_mid
        near_peak, near_am = pk_ref[own[h]], am_ref[own[h]]
        top = jnp.maximum(near_peak, peak_mid)
        out_mid.append(
            jnp.exp2((near_peak - top) * factor) * near_am
            + jnp.exp2((peak_mid - top) * factor) * am_mid[h]
        )
    for h in heads:
        shared = pl.ds(fo[h] // R1, far, stride=R2 // R1)
        also = fo[h] % R1 == mo[h]
        both_peak = jnp.where(also, pk_scr[h, shared], -1e30)
        both_am = am_scr[h, shared]
        near_peak, near_am = pk_ref[own_far[h]], am_ref[own_far[h]]
        top = jnp.maximum(jnp.maximum(near_peak, both_peak), soft_far[h][0])
        out_far.append(
            jnp.exp2((near_peak - top) * factor) * near_am
            + jnp.exp2((both_peak - top) * factor) * both_am
            + jnp.exp2((soft_far[h][0] - top) * factor) * am_far[h]
        )
    for offset, stride, count, out in ((mo, R1, mid, out_mid), (fo, R2, far, out_far)):
        both = pair(out[0], out[1])
        low = lane_half(both.shape)
        for h, keep in ((0, low), (1, jnp.logical_not(low))):
            at = pl.ds(offset[h], count, stride=stride)
            attn_scr[at] = jnp.where(keep, both, attn_scr[at])
        attn_scr[pl.ds(rows + offset[2], count // 2, stride=stride)] = fold(out[2])
    attn_ref[...] = attn_scr[...].astype(bf16)


def output_kernel(head_count, place, x_ref, gb_ref, *rest):
    attns, weights = rest[:head_count], rest[head_count : 2 * head_count]
    out_ref, resid_scr = rest[2 * head_count :]
    rows, width = x_ref.shape
    half = rows // 2
    cols = width // head_count
    low = lane_half((half, LANES))
    w = jnp.concatenate(
        [weights[r][:LANES] for r in range(head_count)]
        + [weights[r][LANES:] for r in range(head_count)],
        axis=0,
    )
    for first in (0, half):
        at = slice(first, first + half)
        tiles = [attns[r][at] for r in range(head_count)]
        for r in range(0, head_count, 2):
            even = attns[r][rows:].astype(f32)
            odd = attns[r + 1][rows:].astype(f32)
            if first == 0:
                joined = jnp.where(low, even, swap(odd))
            else:
                joined = jnp.where(low, swap(even), odd)
            tiles.append(joined.astype(bf16))
        attn = jnp.concatenate(tiles, axis=1)
        resid = x_ref[at].astype(f32) + jnp.dot(attn, w, preferred_element_type=f32)
        mean = jnp.sum(resid, axis=1, keepdims=True) / width
        var = jnp.sum(resid * resid, axis=1, keepdims=True) / width - mean * mean
        resid_scr[at] = (resid - mean) * lax.rsqrt(var + epsilon)
    for i in range(head_count):

        @pl.when(place[0] == i)
        def _():
            mine = resid_scr[:, i * cols : (i + 1) * cols]
            out_ref[...] = (mine * gb_ref[0:1] + gb_ref[1:2]).T.astype(bf16)


IN_VMEM = pl.BlockSpec(memory_space=pltpu.VMEM)
IN_SMEM = pl.BlockSpec(memory_space=pltpu.SMEM)
IN_HBM = pl.BlockSpec(memory_space=pltpu.HBM)


def call(kernel, outs, scratch, scalars, far, near, name, flops, limit):
    return pl.pallas_call(
        kernel,
        out_shape=outs,
        in_specs=[IN_SMEM] * len(scalars) + [IN_HBM] * len(far) + [IN_VMEM] * len(near),
        out_specs=jax.tree.map(lambda _: IN_VMEM, outs),
        scratch_shapes=scratch,
        compiler_params=pltpu.CompilerParams(vmem_limit_bytes=limit << 20),
        name=name,
        cost_estimate=pl.CostEstimate(flops=flops, transcendentals=0, bytes_accessed=4 << 20),
    )(*scalars, *far, *near)


def local(tokens, w_qkv, w_out, gain, bias, mid_offset, far_offset):
    rows, width = tokens.shape
    heads_here = mid_offset.shape[0]
    head_size = width // HEADS
    cols = heads_here * head_size
    factor = math.log2(math.e) / math.sqrt(head_size)
    mid, far = rows // R1, rows // R2
    per = mid + far
    shape = jax.ShapeDtypeStruct
    after = lax.optimization_barrier

    head_count = lax.axis_size("head")
    if head_count & (head_count - 1) == 0:
        paths = [[(i, i ^ r) for i in range(head_count)] for r in range(head_count)]
    else:
        paths = [[(i, (i + r) % head_count) for i in range(head_count)] for r in range(head_count)]

    def to(array, r):
        return lax.ppermute(array, "head", paths[r])

    def spread(array):
        return [array] + [to(array, r) for r in range(1, head_count)]

    two_step = head_count == 4

    qkv, kvp, qp = call(
        project_kernel,
        (
            shape((rows, 5 * LANES), bf16),
            shape((3 * per, LANES), bf16),
            shape((3 * per, LANES), bf16),
        ),
        [
            pltpu.VMEM((rows, width), bf16),
            pltpu.VMEM((3, cols, width), bf16),
            pltpu.VMEM((5, rows, LANES), f32),
            pltpu.SemaphoreType.DMA((4,)),
            pltpu.SemaphoreType.DMA((3, 2)),
        ],
        (mid_offset, far_offset),
        (tokens, jnp.swapaxes(w_qkv, 1, 2)),
        (),
        "project",
        2 * rows * width * 3 * cols,
        56,
    )

    seq_count = lax.axis_size("seq")
    mid_devs = min(8, seq_count)

    def within(step):
        return [
            (i, i // mid_devs * mid_devs + (i + step) % mid_devs) for i in range(seq_count)
        ]

    if mid_devs == seq_count:
        mids = [kvp] + [lax.ppermute(kvp, "seq", within(s)) for s in range(1, mid_devs)]
        fars = None
    else:
        split = kvp.reshape(3, per, LANES)
        piece = split[:, :mid]
        mids = [piece] + [lax.ppermute(piece, "seq", within(s)) for s in range(1, mid_devs)]
        fars = [lax.all_gather(split[:, mid:], "seq", axis=1, tiled=True)]

    if two_step:
        across = to(after((w_out, mids[1]))[0], 2)
        beside = to(after((w_out, mids[1]))[0], 1)
        weights = [w_out, beside, across, to(across, 1)]
    else:
        weights = spread(w_out)

    near, am, pk, gb = call(
        partial(near_kernel, factor),
        (
            shape((rows + rows // 2, LANES), f32),
            shape((3 * per, LANES), f32),
            shape((3 * per, LANES), f32),
            shape((2, cols), f32),
        ),
        [pltpu.VMEM((3, rows, LANES), f32)] * 2,
        (mid_offset, far_offset),
        (),
        (qkv, gain.reshape(1, cols), bias.reshape(1, cols)),
        "near",
        1 << 29,
        24,
    )
    attn = call(
        partial(merge_kernel, factor, len(mids), len(fars or mids)),
        shape((rows + rows // 2, LANES), bf16),
        [pltpu.VMEM((rows + rows // 2, LANES), f32)] + [pltpu.VMEM((3, mid, LANES), f32)] * 2,
        (mid_offset, far_offset),
        (),
        (near, qp, am, pk, *mids, *(fars or mids)),
        "merge",
        1 << 29,
        24,
    )
    if two_step:
        attn_across = to(attn, 2)
        attns = [attn, to(attn, 1), attn_across, to(attn_across, 1)]
    else:
        attns = spread(attn)

    out = call(
        partial(output_kernel, head_count),
        shape((cols, rows), bf16),
        [
            pltpu.VMEM((rows, width), f32),
        ],
        (lax.axis_index("head").reshape(1),),
        (),
        (tokens, gb, *attns, *weights),
        "output",
        2 * rows * width * width,
        24,
    )
    return out.T


def solution(mesh):
    in_specs = (
        P(("group", "seq"), None),
        P(None, None, "head"),
        P("head", None),
        P("head"),
        P("head"),
        P("head"),
        P("head"),
    )
    out_specs = P(("group", "seq"), "head")
    return jax.shard_map(local, mesh=mesh, in_specs=in_specs, out_specs=out_specs, check_vma=False)
```

```python
from functools import partial
import math

import jax
import jax.numpy as jnp
from jax import lax
from jax.experimental import pallas as pl
from jax.experimental.pallas import tpu as pltpu
from jax.sharding import PartitionSpec as P

HEADS = 12
SEG0 = 128
R1 = 8
R2 = 32
LANES = 128
HALF = 64

epsilon = 1e-05
f32 = jnp.float32
bf16 = jnp.bfloat16

NT = (((1,), (1,)), ((), ()))


def lane_half(shape):
    return lax.broadcasted_iota(jnp.int32, shape, 1) < HALF


def acc_low(head):
    return head % 2 == 0


def project_kernel(mo_hbm, fo_hbm, x_hbm, w_hbm, kv_ref, kvp_ref, mo, fo, x_ref, w_ref, scr, sems):
    rows = x_ref.shape[0]
    mid, far = rows // R1, rows // R2
    per = mid + far
    half = rows // 2
    moves = [(w_hbm.at[1], w_ref.at[0]), (w_hbm.at[2], w_ref.at[1])]
    moves += [(x_hbm.at[pl.ds(i * half, half)], x_ref.at[pl.ds(i * half, half)]) for i in range(2)]
    moves += [(mo_hbm, mo), (fo_hbm, fo)]
    copies = [pltpu.make_async_copy(*m, sems.at[i]) for i, m in enumerate(moves)]
    for copy in copies:
        copy.start()
    copies[0].wait()
    copies[1].wait()
    k = [w_ref[0, h * HALF : (h + 1) * HALF] for h in range(3)]
    v = [w_ref[1, h * HALF : (h + 1) * HALF] for h in range(3)]
    w = jnp.concatenate([v[0], k[0], k[1], v[1], v[2], k[2]], axis=0)
    for i in range(2):
        copies[2 + i].wait()
        at = slice(i * half, (i + 1) * half)
        y = lax.dot_general(x_ref[at], w, NT, preferred_element_type=f32).astype(bf16)
        kv_ref[at] = y
        for h in range(3):
            scr[h, at] = y[:, h * LANES : (h + 1) * LANES].astype(f32)
    copies[4].wait()
    copies[5].wait()
    for h in range(3):
        mid_rows = pl.ds(mo[h], mid, stride=R1)
        far_rows = pl.ds(fo[h], far, stride=R2)
        kvp_ref[h * per : h * per + mid] = scr[h, mid_rows].astype(bf16)
        kvp_ref[h * per + mid : (h + 1) * per] = scr[h, far_rows].astype(bf16)


def scores(queries, keys_values):
    return lax.dot_general(queries, keys_values, NT, preferred_element_type=f32)


def soften(s, factor):
    peak = jnp.max(s, axis=1, keepdims=True)
    return peak, jnp.exp2((s - peak) * factor).astype(bf16)


def weigh(p, keys_values, head):
    low = lane_half(keys_values.shape)
    is_value = low if acc_low(head) else jnp.logical_not(low)
    values = jnp.where(is_value, keys_values, jnp.ones((), bf16))
    return jnp.dot(p, values, preferred_element_type=f32)


def swap(x):
    return pltpu.roll(x, HALF, 1)


def pair(a, b):
    low = lane_half(a.shape)
    return jnp.where(low, a, b) / swap(jnp.where(low, b, a))


def fold(x):
    half = x.shape[0] // 2
    a, b = x[:half], x[half:]
    low = lane_half(a.shape)
    return jnp.where(low, a, swap(b)) / jnp.where(low, swap(a), b)


def near_kernel(
    factor,
    mo,
    fo,
    w_hbm,
    kv_ref,
    x_ref,
    gain_ref,
    bias_ref,
    near_ref,
    am_ref,
    pk_ref,
    qp_ref,
    gb_ref,
    am_scr,
    pk_scr,
    q_scr,
    q_ref,
    w_ref,
    sem,
):
    copy = pltpu.make_async_copy(w_hbm.at[0], w_ref, sem)
    copy.start()
    gb_ref[0:1] = gain_ref[...]
    gb_ref[1:2] = bias_ref[...]
    rows = kv_ref.shape[0]
    mid, far = rows // R1, rows // R2
    per = mid + far
    low = lane_half((SEG0, LANES))
    blocks = rows // SEG0
    units = [(b, h) for b in range(blocks) for h in range(3)]
    copy.wait()
    q = [w_ref[h * HALF : (h + 1) * HALF] for h in range(3)]
    w = jnp.concatenate([q[1], q[0], q[2], q[2]], axis=0)
    y = lax.dot_general(x_ref[...], w, NT, preferred_element_type=f32).astype(bf16)
    q_ref[...] = y
    for i in range(2):
        q_scr[i] = y[:, i * LANES : (i + 1) * LANES].astype(f32)

    def rows_of(b):
        return slice(b * SEG0, (b + 1) * SEG0)

    def kv(b, h):
        return kv_ref[rows_of(b), h * LANES : (h + 1) * LANES]

    def ask(b, h):
        keep = jnp.logical_not(low) if acc_low(h) else low
        first = h // 2 * LANES
        q = q_ref[rows_of(b), first : first + LANES]
        return scores(jnp.where(keep, q, jnp.zeros((), bf16)), kv(b, h))

    s = {u: ask(*u) for u in units[:3]}
    am = {}
    for i, u in enumerate(units):
        if i + 3 < len(units):
            s[units[i + 3]] = ask(*units[i + 3])
        b, h = u
        peak, p = soften(s.pop(u), factor)
        am[u] = weigh(p, kv(b, h), h)
        am_scr[h, rows_of(b)] = am[u]
        pk_scr[h, rows_of(b)] = jnp.broadcast_to(peak, am[u].shape)
        if h == 2:
            near_ref[rows_of(b)] = pair(am.pop((b, 0)), am.pop((b, 1)))
    near_ref[rows:] = fold(am_scr[2])
    for h in range(3):
        own, own_far = slice(h * per, h * per + mid), slice(h * per + mid, (h + 1) * per)
        mid_rows = pl.ds(mo[h], mid, stride=R1)
        far_rows = pl.ds(fo[h], far, stride=R2)
        am_ref[own], am_ref[own_far] = am_scr[h, mid_rows], am_scr[h, far_rows]
        pk_ref[own], pk_ref[own_far] = pk_scr[h, mid_rows], pk_scr[h, far_rows]
        keep = lane_half((mid, LANES))
        keep = jnp.logical_not(keep) if acc_low(h) else keep
        for at, picked, kept in ((own, mid_rows, keep), (own_far, far_rows, keep[:far])):
            qp_ref[at] = jnp.where(kept, q_scr[h // 2, picked], 0.0).astype(bf16)


def merge_kernel(factor, mid_n, far_n, mo, fo, near_ref, qp_ref, am_ref, pk_ref, *rest):
    mids, fars = rest[:mid_n], rest[mid_n : mid_n + far_n]
    attn_ref, attn_scr, am_scr, pk_scr = rest[mid_n + far_n :]
    rows = near_ref.shape[0] * 2 // 3
    attn_scr[...] = near_ref[...]
    per = qp_ref.shape[0] // 3
    far = per * R1 // (R1 + R2)
    mid = per - far
    heads = range(3)
    own = [slice(h * per, h * per + mid) for h in heads]
    own_far = [slice(h * per + mid, (h + 1) * per) for h in heads]

    def joined(refs, h, whole, at):
        return jnp.concatenate([m[at[h]] if m.shape[0] == 3 * per else m[h] for m in refs], axis=0)

    kv_mid = [joined(mids, h, per, own) for h in heads]
    kv_far = [joined(fars, h, per, own_far) for h in heads]
    s_mid = [scores(qp_ref[own[h]], kv_mid[h]) for h in heads]
    s_far = [scores(qp_ref[own_far[h]], kv_far[h]) for h in heads]
    soft_mid = [soften(s, factor) for s in s_mid]
    soft_far = [soften(s, factor) for s in s_far]
    am_mid = [weigh(soft_mid[h][1], kv_mid[h], h) for h in heads]
    am_far = [weigh(soft_far[h][1], kv_far[h], h) for h in heads]
    out_mid, out_far = [], []
    for h in heads:
        peak_mid = jnp.broadcast_to(soft_mid[h][0], am_mid[h].shape)
        am_scr[h] = am_mid[h]
        pk_scr[h] = peak_mid
        near_peak, near_am = pk_ref[own[h]], am_ref[own[h]]
        top = jnp.maximum(near_peak, peak_mid)
        out_mid.append(
            jnp.exp2((near_peak - top) * factor) * near_am
            + jnp.exp2((peak_mid - top) * factor) * am_mid[h]
        )
    for h in heads:
        shared = pl.ds(fo[h] // R1, far, stride=R2 // R1)
        also = fo[h] % R1 == mo[h]
        both_peak = jnp.where(also, pk_scr[h, shared], -1e30)
        both_am = am_scr[h, shared]
        near_peak, near_am = pk_ref[own_far[h]], am_ref[own_far[h]]
        top = jnp.maximum(jnp.maximum(near_peak, both_peak), soft_far[h][0])
        out_far.append(
            jnp.exp2((near_peak - top) * factor) * near_am
            + jnp.exp2((both_peak - top) * factor) * both_am
            + jnp.exp2((soft_far[h][0] - top) * factor) * am_far[h]
        )
    for offset, stride, count, out in ((mo, R1, mid, out_mid), (fo, R2, far, out_far)):
        both = pair(out[0], out[1])
        low = lane_half(both.shape)
        for h, keep in ((0, low), (1, jnp.logical_not(low))):
            at = pl.ds(offset[h], count, stride=stride)
            attn_scr[at] = jnp.where(keep, both, attn_scr[at])
        attn_scr[pl.ds(rows + offset[2], count // 2, stride=stride)] = fold(out[2])
    attn_ref[...] = attn_scr[...].astype(bf16)


def output_kernel(head_count, place, x_ref, gb_ref, *rest):
    attns, weights = rest[:head_count], rest[head_count : 2 * head_count]
    out_ref, resid_scr = rest[2 * head_count :]
    rows, width = x_ref.shape
    half = rows // 2
    cols = width // head_count
    low = lane_half((half, LANES))
    w = jnp.concatenate(
        [weights[r][:LANES] for r in range(head_count)]
        + [weights[r][LANES:] for r in range(head_count)],
        axis=0,
    )
    for first in (0, half):
        at = slice(first, first + half)
        tiles = [attns[r][at] for r in range(head_count)]
        for r in range(0, head_count, 2):
            even = attns[r][rows:].astype(f32)
            odd = attns[r + 1][rows:].astype(f32)
            if first == 0:
                joined = jnp.where(low, even, swap(odd))
            else:
                joined = jnp.where(low, swap(even), odd)
            tiles.append(joined.astype(bf16))
        attn = jnp.concatenate(tiles, axis=1)
        resid = x_ref[at].astype(f32) + jnp.dot(attn, w, preferred_element_type=f32)
        mean = jnp.sum(resid, axis=1, keepdims=True) / width
        var = jnp.sum(resid * resid, axis=1, keepdims=True) / width - mean * mean
        resid_scr[at] = (resid - mean) * lax.rsqrt(var + epsilon)
    for i in range(head_count):

        @pl.when(place[0] == i)
        def _():
            mine = resid_scr[:, i * cols : (i + 1) * cols]
            out_ref[...] = (mine * gb_ref[0:1] + gb_ref[1:2]).T.astype(bf16)


IN_VMEM = pl.BlockSpec(memory_space=pltpu.VMEM)
IN_SMEM = pl.BlockSpec(memory_space=pltpu.SMEM)
IN_HBM = pl.BlockSpec(memory_space=pltpu.HBM)


def call(kernel, outs, scratch, scalars, far, near, name, flops, limit):
    return pl.pallas_call(
        kernel,
        out_shape=outs,
        in_specs=[IN_SMEM] * len(scalars) + [IN_HBM] * len(far) + [IN_VMEM] * len(near),
        out_specs=jax.tree.map(lambda _: IN_VMEM, outs),
        scratch_shapes=scratch,
        compiler_params=pltpu.CompilerParams(vmem_limit_bytes=limit << 20),
        name=name,
        cost_estimate=pl.CostEstimate(flops=flops, transcendentals=0, bytes_accessed=4 << 20),
    )(*scalars, *far, *near)


def local(tokens, w_qkv, w_out, gain, bias, mid_offset, far_offset):
    rows, width = tokens.shape
    heads_here = mid_offset.shape[0]
    head_size = width // HEADS
    cols = heads_here * head_size
    factor = math.log2(math.e) / math.sqrt(head_size)
    mid, far = rows // R1, rows // R2
    per = mid + far
    shape = jax.ShapeDtypeStruct
    after = lax.optimization_barrier

    head_count = lax.axis_size("head")
    if head_count & (head_count - 1) == 0:
        paths = [[(i, i ^ r) for i in range(head_count)] for r in range(head_count)]
    else:
        paths = [[(i, (i + r) % head_count) for i in range(head_count)] for r in range(head_count)]

    def to(array, r):
        return lax.ppermute(array, "head", paths[r])

    def spread(array):
        return [array] + [to(array, r) for r in range(1, head_count)]

    two_step = head_count == 4

    def pinned(array):
        return pltpu.with_memory_space_constraint(array, pltpu.HBM)

    w_rows = pinned(jnp.swapaxes(w_qkv, 1, 2))
    kv, kvp = call(
        project_kernel,
        (shape((rows, 3 * LANES), bf16), shape((3 * per, LANES), bf16)),
        [
            pltpu.SMEM((heads_here,), jnp.int32),
            pltpu.SMEM((heads_here,), jnp.int32),
            pltpu.VMEM((rows, width), bf16),
            pltpu.VMEM((2, cols, width), bf16),
            pltpu.VMEM((3, rows, LANES), f32),
            pltpu.SemaphoreType.DMA((6,)),
        ],
        (),
        (pinned(mid_offset), pinned(far_offset), pinned(tokens), w_rows),
        (),
        "project",
        2 * rows * width * 2 * cols,
        24,
    )

    seq_count = lax.axis_size("seq")
    mid_devs = min(8, seq_count)

    def within(step):
        return [
            (i, i // mid_devs * mid_devs + (i + step) % mid_devs) for i in range(seq_count)
        ]

    if mid_devs == seq_count:
        mids = [kvp] + [lax.ppermute(kvp, "seq", within(s)) for s in range(1, mid_devs)]
        fars = None
    else:
        split = kvp.reshape(3, per, LANES)
        piece = split[:, :mid]
        mids = [piece] + [lax.ppermute(piece, "seq", within(s)) for s in range(1, mid_devs)]
        fars = [lax.all_gather(split[:, mid:], "seq", axis=1, tiled=True)]

    if two_step:
        across = to(after((w_out, kvp))[0], 2)
        beside = to(after((w_out, kvp))[0], 1)
        weights = [w_out, beside, across, to(across, 1)]
    else:
        weights = spread(w_out)

    near, am, pk, qp, gb = call(
        partial(near_kernel, factor),
        (
            shape((rows + rows // 2, LANES), f32),
            shape((3 * per, LANES), f32),
            shape((3 * per, LANES), f32),
            shape((3 * per, LANES), bf16),
            shape((2, cols), f32),
        ),
        [
            pltpu.VMEM((3, rows, LANES), f32),
            pltpu.VMEM((3, rows, LANES), f32),
            pltpu.VMEM((2, rows, LANES), f32),
            pltpu.VMEM((rows, 2 * LANES), bf16),
            pltpu.VMEM((cols, width), bf16),
            pltpu.SemaphoreType.DMA(()),
        ],
        (mid_offset, far_offset),
        (w_rows,),
        (kv, tokens, gain.reshape(1, cols), bias.reshape(1, cols)),
        "near",
        1 << 29,
        24,
    )
    attn = call(
        partial(merge_kernel, factor, len(mids), len(fars or mids)),
        shape((rows + rows // 2, LANES), bf16),
        [pltpu.VMEM((rows + rows // 2, LANES), f32)] + [pltpu.VMEM((3, mid, LANES), f32)] * 2,
        (mid_offset, far_offset),
        (),
        (near, qp, am, pk, *mids, *(fars or mids)),
        "merge",
        1 << 29,
        24,
    )
    if two_step:
        attn_across = to(attn, 2)
        attns = [attn, to(attn, 1), attn_across, to(attn_across, 1)]
    else:
        attns = spread(attn)

    out = call(
        partial(output_kernel, head_count),
        shape((cols, rows), bf16),
        [
            pltpu.VMEM((rows, width), f32),
        ],
        (lax.axis_index("head").reshape(1),),
        (),
        (tokens, gb, *attns, *weights),
        "output",
        2 * rows * width * width,
        24,
    )
    return out.T


def solution(mesh):
    in_specs = (
        P(("group", "seq"), None),
        P(None, None, "head"),
        P("head", None),
        P("head"),
        P("head"),
        P("head"),
        P("head"),
    )
    out_specs = P(("group", "seq"), "head")
    return jax.shard_map(local, mesh=mesh, in_specs=in_specs, out_specs=out_specs, check_vma=False)
```

```python
from functools import partial
import math

import jax
import jax.numpy as jnp
from jax import lax
from jax.experimental import pallas as pl
from jax.experimental.pallas import tpu as pltpu
from jax.sharding import PartitionSpec as P

HEADS = 12
SEG0 = 128
R1 = 8
R2 = 32
LANES = 128
HALF = 64

epsilon = 1e-05
f32 = jnp.float32
bf16 = jnp.bfloat16

NT = (((1,), (1,)), ((), ()))


def lane_half(shape):
    return lax.broadcasted_iota(jnp.int32, shape, 1) < HALF


def acc_low(head):
    return head % 2 == 0


def project_kernel(
    mo_hbm, fo_hbm, x_hbm, w_hbm, kv_ref, kvp_ref, x_ref, wq_ref, mo, fo, w_ref, scr, sems
):
    rows = x_ref.shape[0]
    mid, far = rows // R1, rows // R2
    per = mid + far
    half = rows // 2
    moves = [(w_hbm.at[1], w_ref.at[0]), (w_hbm.at[2], w_ref.at[1])]
    moves += [(x_hbm.at[pl.ds(i * half, half)], x_ref.at[pl.ds(i * half, half)]) for i in range(2)]
    moves += [(mo_hbm, mo), (fo_hbm, fo), (w_hbm.at[0], wq_ref)]
    copies = [pltpu.make_async_copy(*m, sems.at[i]) for i, m in enumerate(moves)]
    for copy in copies:
        copy.start()
    copies[0].wait()
    copies[1].wait()
    k = [w_ref[0, h * HALF : (h + 1) * HALF] for h in range(3)]
    v = [w_ref[1, h * HALF : (h + 1) * HALF] for h in range(3)]
    w = jnp.concatenate([v[0], k[0], k[1], v[1], v[2], k[2]], axis=0)
    for i in range(2):
        copies[2 + i].wait()
        at = slice(i * half, (i + 1) * half)
        y = lax.dot_general(x_ref[at], w, NT, preferred_element_type=f32).astype(bf16)
        kv_ref[at] = y
        for h in range(3):
            scr[h, at] = y[:, h * LANES : (h + 1) * LANES].astype(f32)
    copies[4].wait()
    copies[5].wait()
    for h in range(3):
        mid_rows = pl.ds(mo[h], mid, stride=R1)
        far_rows = pl.ds(fo[h], far, stride=R2)
        kvp_ref[h * per : h * per + mid] = scr[h, mid_rows].astype(bf16)
        kvp_ref[h * per + mid : (h + 1) * per] = scr[h, far_rows].astype(bf16)
    copies[6].wait()


def scores(queries, keys_values):
    return lax.dot_general(queries, keys_values, NT, preferred_element_type=f32)


def soften(s, factor):
    peak = jnp.max(s, axis=1, keepdims=True)
    return peak, jnp.exp2((s - peak) * factor).astype(bf16)


def weigh(p, keys_values, head):
    low = lane_half(keys_values.shape)
    is_value = low if acc_low(head) else jnp.logical_not(low)
    values = jnp.where(is_value, keys_values, jnp.ones((), bf16))
    return jnp.dot(p, values, preferred_element_type=f32)


def swap(x):
    return pltpu.roll(x, HALF, 1)


def pair(a, b):
    low = lane_half(a.shape)
    return jnp.where(low, a, b) / swap(jnp.where(low, b, a))


def fold(x):
    half = x.shape[0] // 2
    a, b = x[:half], x[half:]
    low = lane_half(a.shape)
    return jnp.where(low, a, swap(b)) / jnp.where(low, swap(a), b)


def tell(mo_hbm, fo_hbm, mo, fo, sems):
    copies = [
        pltpu.make_async_copy(mo_hbm, mo, sems.at[0]),
        pltpu.make_async_copy(fo_hbm, fo, sems.at[1]),
    ]
    for copy in copies:
        copy.start()
    return copies


def near_kernel(
    factor,
    mo_hbm,
    fo_hbm,
    kv_ref,
    x_ref,
    w_ref,
    gain_ref,
    bias_ref,
    near_ref,
    am_ref,
    pk_ref,
    qp_ref,
    gb_ref,
    mo,
    fo,
    am_scr,
    pk_scr,
    q_scr,
    q_ref,
    sems,
):
    copies = tell(mo_hbm, fo_hbm, mo, fo, sems)
    gb_ref[0:1] = gain_ref[...]
    gb_ref[1:2] = bias_ref[...]
    rows = kv_ref.shape[0]
    mid, far = rows // R1, rows // R2
    per = mid + far
    low = lane_half((SEG0, LANES))
    blocks = rows // SEG0
    units = [(b, h) for b in range(blocks) for h in range(3)]
    q = [w_ref[h * HALF : (h + 1) * HALF] for h in range(3)]
    w = jnp.concatenate([q[1], q[0], q[2], q[2]], axis=0)
    y = lax.dot_general(x_ref[...], w, NT, preferred_element_type=f32).astype(bf16)
    q_ref[...] = y
    for i in range(2):
        q_scr[i] = y[:, i * LANES : (i + 1) * LANES].astype(f32)

    def rows_of(b):
        return slice(b * SEG0, (b + 1) * SEG0)

    def kv(b, h):
        return kv_ref[rows_of(b), h * LANES : (h + 1) * LANES]

    def ask(b, h):
        keep = jnp.logical_not(low) if acc_low(h) else low
        first = h // 2 * LANES
        q = q_ref[rows_of(b), first : first + LANES]
        return scores(jnp.where(keep, q, jnp.zeros((), bf16)), kv(b, h))

    s = {u: ask(*u) for u in units[:3]}
    am = {}
    for i, u in enumerate(units):
        if i + 3 < len(units):
            s[units[i + 3]] = ask(*units[i + 3])
        b, h = u
        peak, p = soften(s.pop(u), factor)
        am[u] = weigh(p, kv(b, h), h)
        am_scr[h, rows_of(b)] = am[u]
        pk_scr[h, rows_of(b)] = jnp.broadcast_to(peak, am[u].shape)
        if h == 2:
            near_ref[rows_of(b)] = pair(am.pop((b, 0)), am.pop((b, 1)))
    near_ref[rows:] = fold(am_scr[2])
    for copy in copies:
        copy.wait()
    for h in range(3):
        own, own_far = slice(h * per, h * per + mid), slice(h * per + mid, (h + 1) * per)
        mid_rows = pl.ds(mo[h], mid, stride=R1)
        far_rows = pl.ds(fo[h], far, stride=R2)
        am_ref[own], am_ref[own_far] = am_scr[h, mid_rows], am_scr[h, far_rows]
        pk_ref[own], pk_ref[own_far] = pk_scr[h, mid_rows], pk_scr[h, far_rows]
        keep = lane_half((mid, LANES))
        keep = jnp.logical_not(keep) if acc_low(h) else keep
        for at, picked, kept in ((own, mid_rows, keep), (own_far, far_rows, keep[:far])):
            qp_ref[at] = jnp.where(kept, q_scr[h // 2, picked], 0.0).astype(bf16)


def merge_kernel(factor, mid_n, far_n, mo_hbm, fo_hbm, near_ref, qp_ref, am_ref, pk_ref, *rest):
    mids, fars = rest[:mid_n], rest[mid_n : mid_n + far_n]
    attn_ref, mo, fo, attn_scr, am_scr, pk_scr, sems = rest[mid_n + far_n :]
    copies = tell(mo_hbm, fo_hbm, mo, fo, sems)
    rows = near_ref.shape[0] * 2 // 3
    attn_scr[...] = near_ref[...]
    per = qp_ref.shape[0] // 3
    far = per * R1 // (R1 + R2)
    mid = per - far
    heads = range(3)
    own = [slice(h * per, h * per + mid) for h in heads]
    own_far = [slice(h * per + mid, (h + 1) * per) for h in heads]

    def joined(refs, h, whole, at):
        return jnp.concatenate([m[at[h]] if m.shape[0] == 3 * per else m[h] for m in refs], axis=0)

    kv_mid = [joined(mids, h, per, own) for h in heads]
    kv_far = [joined(fars, h, per, own_far) for h in heads]
    s_mid = [scores(qp_ref[own[h]], kv_mid[h]) for h in heads]
    s_far = [scores(qp_ref[own_far[h]], kv_far[h]) for h in heads]
    soft_mid = [soften(s, factor) for s in s_mid]
    soft_far = [soften(s, factor) for s in s_far]
    am_mid = [weigh(soft_mid[h][1], kv_mid[h], h) for h in heads]
    am_far = [weigh(soft_far[h][1], kv_far[h], h) for h in heads]
    out_mid, out_far = [], []
    for h in heads:
        peak_mid = jnp.broadcast_to(soft_mid[h][0], am_mid[h].shape)
        am_scr[h] = am_mid[h]
        pk_scr[h] = peak_mid
        near_peak, near_am = pk_ref[own[h]], am_ref[own[h]]
        top = jnp.maximum(near_peak, peak_mid)
        out_mid.append(
            jnp.exp2((near_peak - top) * factor) * near_am
            + jnp.exp2((peak_mid - top) * factor) * am_mid[h]
        )
    for copy in copies:
        copy.wait()
    for h in heads:
        shared = pl.ds(fo[h] // R1, far, stride=R2 // R1)
        also = fo[h] % R1 == mo[h]
        both_peak = jnp.where(also, pk_scr[h, shared], -1e30)
        both_am = am_scr[h, shared]
        near_peak, near_am = pk_ref[own_far[h]], am_ref[own_far[h]]
        top = jnp.maximum(jnp.maximum(near_peak, both_peak), soft_far[h][0])
        out_far.append(
            jnp.exp2((near_peak - top) * factor) * near_am
            + jnp.exp2((both_peak - top) * factor) * both_am
            + jnp.exp2((soft_far[h][0] - top) * factor) * am_far[h]
        )
    for offset, stride, count, out in ((mo, R1, mid, out_mid), (fo, R2, far, out_far)):
        both = pair(out[0], out[1])
        low = lane_half(both.shape)
        for h, keep in ((0, low), (1, jnp.logical_not(low))):
            at = pl.ds(offset[h], count, stride=stride)
            attn_scr[at] = jnp.where(keep, both, attn_scr[at])
        attn_scr[pl.ds(rows + offset[2], count // 2, stride=stride)] = fold(out[2])
    attn_ref[...] = attn_scr[...].astype(bf16)


def product(first, half, attns, weights):
    total = None
    for attn, weight in zip(attns, weights):
        third = attn[2 * half :]
        if first:
            third = swap(third.astype(f32)).astype(bf16)
        rows = jnp.concatenate([attn[first : first + half], third[:, :HALF]], axis=1)
        part = jnp.dot(rows, weight[...], preferred_element_type=f32)
        total = part if total is None else total + part
    return total


def product_kernel(x_ref, *rest):
    out_ref, count = rest[-1], len(rest) // 2
    half = x_ref.shape[0] // 2
    for first in (0, half):
        at = slice(first, first + half)
        part = product(first, half, rest[:count], rest[count : 2 * count])
        out_ref[at] = x_ref[at].astype(f32) + part


def output_kernel(head_count, place, x_ref, gb_ref, *rest):
    out_ref, resid_scr = rest[-2:]
    count = len(rest) // 2 - 1
    rows, width = x_ref.shape
    half = rows // 2
    cols = width // head_count
    for first in (0, half):
        at = slice(first, first + half)
        resid = x_ref[at].astype(f32) + product(first, half, rest[:count], rest[count : 2 * count])
        mean = jnp.sum(resid, axis=1, keepdims=True) / width
        var = jnp.sum(resid * resid, axis=1, keepdims=True) / width - mean * mean
        resid_scr[at] = (resid - mean) * lax.rsqrt(var + epsilon)
    for i in range(head_count):

        @pl.when(place[0] == i)
        def _():
            mine = resid_scr[:, i * cols : (i + 1) * cols]
            out_ref[...] = (mine * gb_ref[0:1] + gb_ref[1:2]).T.astype(bf16)


IN_VMEM = pl.BlockSpec(memory_space=pltpu.VMEM)
IN_SMEM = pl.BlockSpec(memory_space=pltpu.SMEM)
IN_HBM = pl.BlockSpec(memory_space=pltpu.HBM)


def call(kernel, outs, scratch, scalars, far, near, name, flops, limit):
    return pl.pallas_call(
        kernel,
        out_shape=outs,
        in_specs=[IN_SMEM] * len(scalars) + [IN_HBM] * len(far) + [IN_VMEM] * len(near),
        out_specs=jax.tree.map(lambda _: IN_VMEM, outs),
        scratch_shapes=scratch,
        compiler_params=pltpu.CompilerParams(vmem_limit_bytes=limit << 20),
        name=name,
        cost_estimate=pl.CostEstimate(flops=flops, transcendentals=0, bytes_accessed=4 << 20),
    )(*scalars, *far, *near)


def local(tokens, w_qkv, w_out, gain, bias, mid_offset, far_offset):
    rows, width = tokens.shape
    heads_here = mid_offset.shape[0]
    head_size = width // HEADS
    cols = heads_here * head_size
    factor = math.log2(math.e) / math.sqrt(head_size)
    mid, far = rows // R1, rows // R2
    per = mid + far
    shape = jax.ShapeDtypeStruct
    after = lax.optimization_barrier

    head_count = lax.axis_size("head")
    if head_count & (head_count - 1) == 0:
        paths = [[(i, i ^ r) for i in range(head_count)] for r in range(head_count)]
    else:
        paths = [[(i, (i + r) % head_count) for i in range(head_count)] for r in range(head_count)]

    def to(array, r):
        return lax.ppermute(array, "head", paths[r])

    def spread(array):
        return [array] + [to(array, r) for r in range(1, head_count)]

    two_step = head_count == 4

    def pinned(array):
        return pltpu.with_memory_space_constraint(array, pltpu.HBM)

    w_rows = pinned(jnp.swapaxes(w_qkv, 1, 2))
    offsets = (pinned(mid_offset), pinned(far_offset))
    told = [pltpu.SMEM((heads_here,), jnp.int32)] * 2
    kv, kvp, x, w_query = call(
        project_kernel,
        (
            shape((rows, 3 * LANES), bf16),
            shape((3 * per, LANES), bf16),
            shape((rows, width), bf16),
            shape((cols, width), bf16),
        ),
        [
            *told,
            pltpu.VMEM((2, cols, width), bf16),
            pltpu.VMEM((3, rows, LANES), f32),
            pltpu.SemaphoreType.DMA((7,)),
        ],
        (),
        (*offsets, pinned(tokens), w_rows),
        (),
        "project",
        2 * rows * width * 2 * cols,
        24,
    )

    seq_count = lax.axis_size("seq")
    mid_devs = min(8, seq_count)

    def within(step):
        def partner(i):
            if mid_devs & (mid_devs - 1) == 0:
                return i % mid_devs ^ step
            return (i + step) % mid_devs

        return [(i, i // mid_devs * mid_devs + partner(i)) for i in range(seq_count)]

    if mid_devs == seq_count:
        mids = [kvp] + [lax.ppermute(kvp, "seq", within(s)) for s in range(mid_devs - 1, 0, -1)]
        fars = None
    else:
        split = kvp.reshape(3, per, LANES)
        piece = split[:, :mid]
        mids = [piece] + [lax.ppermute(piece, "seq", within(s)) for s in range(mid_devs - 1, 0, -1)]
        fars = [lax.all_gather(split[:, mid:], "seq", axis=1, tiled=True)]

    if two_step:
        across = to(after((w_out, kvp))[0], 2)
        beside = to(after((w_out, kvp))[0], 1)
        weights = [w_out, beside, across, to(across, 1)]
    else:
        weights = spread(w_out)

    near, am, pk, qp, gb = call(
        partial(near_kernel, factor),
        (
            shape((rows + rows // 2, LANES), f32),
            shape((3 * per, LANES), f32),
            shape((3 * per, LANES), f32),
            shape((3 * per, LANES), bf16),
            shape((2, cols), f32),
        ),
        [
            *told,
            pltpu.VMEM((3, rows, LANES), f32),
            pltpu.VMEM((3, rows, LANES), f32),
            pltpu.VMEM((2, rows, LANES), f32),
            pltpu.VMEM((rows, 2 * LANES), bf16),
            pltpu.SemaphoreType.DMA((2,)),
        ],
        (),
        offsets,
        (kv, x, w_query, gain.reshape(1, cols), bias.reshape(1, cols)),
        "near",
        1 << 29,
        24,
    )
    attn = call(
        partial(merge_kernel, factor, len(mids), len(fars or mids)),
        shape((rows + rows // 2, LANES), bf16),
        [
            *told,
            pltpu.VMEM((rows + rows // 2, LANES), f32),
            pltpu.VMEM((3, mid, LANES), f32),
            pltpu.VMEM((3, mid, LANES), f32),
            pltpu.SemaphoreType.DMA((2,)),
        ],
        (),
        offsets,
        (near, qp, am, pk, *mids, *(fars or mids)),
        "merge",
        1 << 29,
        24,
    )
    def add(base, *which):
        return call(
            product_kernel,
            shape((rows, width), f32),
            [],
            (),
            (),
            (base, *(attns[i] for i in which), *(weights[i] for i in which)),
            "product",
            len(which) * 2 * rows * cols * width,
            24,
        )

    resid = x
    if two_step:
        attns = [attn, to(attn, 1), to(attn, 2)]
        resid = add(resid, 0, 1)
        resid, attns[2] = after((resid, attns[2]))
        attns.append(to(attns[2], 1))
        resid = add(resid, 2)
    else:
        attns = spread(attn)
    left = slice(3, None) if two_step else slice(None)
    out = call(
        partial(output_kernel, head_count),
        shape((cols, rows), bf16),
        [pltpu.VMEM((rows, width), f32)],
        (lax.axis_index("head").reshape(1),),
        (),
        (resid, gb, *attns[left], *weights[left]),
        "output",
        2 * rows * width * cols,
        24,
    )
    return out.T


def solution(mesh):
    in_specs = (
        P(("group", "seq"), None),
        P(None, None, "head"),
        P("head", None),
        P("head"),
        P("head"),
        P("head"),
        P("head"),
    )
    out_specs = P(("group", "seq"), "head")
    return jax.shard_map(local, mesh=mesh, in_specs=in_specs, out_specs=out_specs, check_vma=False)
```

```python
from functools import partial
import math

import jax
import jax.numpy as jnp
from jax import lax
from jax.experimental import pallas as pl
from jax.experimental.pallas import tpu as pltpu
from jax.sharding import PartitionSpec as P

HEADS = 12
SEG0 = 128
R1 = 8
R2 = 32
LANES = 128
HALF = 64

epsilon = 1e-05
f32 = jnp.float32
bf16 = jnp.bfloat16

NT = (((1,), (1,)), ((), ()))


def lane_half(shape):
    return lax.broadcasted_iota(jnp.int32, shape, 1) < HALF


def acc_low(head):
    return head % 2 == 0


def project_kernel(
    mo_hbm, fo_hbm, x_hbm, w_hbm, kv_ref, kvp_ref, x_ref, wq_ref, mo, fo, w_ref, scr, sems
):
    rows = x_ref.shape[0]
    mid, far = rows // R1, rows // R2
    per = mid + far
    half = rows // 2
    moves = [(w_hbm.at[1], w_ref.at[0]), (w_hbm.at[2], w_ref.at[1])]
    moves += [(x_hbm.at[pl.ds(i * half, half)], x_ref.at[pl.ds(i * half, half)]) for i in range(2)]
    moves += [(mo_hbm, mo), (fo_hbm, fo), (w_hbm.at[0], wq_ref)]
    copies = [pltpu.make_async_copy(*m, sems.at[i]) for i, m in enumerate(moves)]
    for copy in copies:
        copy.start()
    copies[0].wait()
    copies[1].wait()
    k = [w_ref[0, h * HALF : (h + 1) * HALF] for h in range(3)]
    v = [w_ref[1, h * HALF : (h + 1) * HALF] for h in range(3)]
    w = jnp.concatenate([v[0], k[0], k[1], v[1], v[2], k[2]], axis=0)
    for i in range(2):
        copies[2 + i].wait()
        at = slice(i * half, (i + 1) * half)
        y = lax.dot_general(x_ref[at], w, NT, preferred_element_type=f32).astype(bf16)
        kv_ref[at] = y
        for h in range(3):
            scr[h, at] = y[:, h * LANES : (h + 1) * LANES].astype(f32)
    copies[4].wait()
    copies[5].wait()
    for h in range(3):
        mid_rows = pl.ds(mo[h], mid, stride=R1)
        far_rows = pl.ds(fo[h], far, stride=R2)
        kvp_ref[h * per : h * per + mid] = scr[h, mid_rows].astype(bf16)
        kvp_ref[h * per + mid : (h + 1) * per] = scr[h, far_rows].astype(bf16)
    copies[6].wait()


def scores(queries, keys_values):
    return lax.dot_general(queries, keys_values, NT, preferred_element_type=f32)


def soften(s, factor):
    peak = jnp.max(s, axis=1, keepdims=True)
    return peak, jnp.exp2((s - peak) * factor).astype(bf16)


def weigh(p, keys_values, head):
    low = lane_half(keys_values.shape)
    is_value = low if acc_low(head) else jnp.logical_not(low)
    values = jnp.where(is_value, keys_values, jnp.ones((), bf16))
    return jnp.dot(p, values, preferred_element_type=f32)


def swap(x):
    return pltpu.roll(x, HALF, 1)


def pair(a, b):
    low = lane_half(a.shape)
    return jnp.where(low, a, b) / swap(jnp.where(low, b, a))


def fold(x):
    half = x.shape[0] // 2
    a, b = x[:half], x[half:]
    low = lane_half(a.shape)
    return jnp.where(low, a, swap(b)) / jnp.where(low, swap(a), b)


def tell(mo_hbm, fo_hbm, mo, fo, sems):
    copies = [
        pltpu.make_async_copy(mo_hbm, mo, sems.at[0]),
        pltpu.make_async_copy(fo_hbm, fo, sems.at[1]),
    ]
    for copy in copies:
        copy.start()
    return copies


def near_kernel(
    factor,
    mo_hbm,
    fo_hbm,
    kv_ref,
    x_ref,
    w_ref,
    gain_ref,
    bias_ref,
    near_ref,
    am_ref,
    pk_ref,
    qp_ref,
    gb_ref,
    mo,
    fo,
    am_scr,
    pk_scr,
    q_scr,
    q_ref,
    sems,
):
    copies = tell(mo_hbm, fo_hbm, mo, fo, sems)
    gb_ref[0:1] = gain_ref[...]
    gb_ref[1:2] = bias_ref[...]
    rows = kv_ref.shape[0]
    mid, far = rows // R1, rows // R2
    per = mid + far
    low = lane_half((SEG0, LANES))
    blocks = rows // SEG0
    units = [(b, h) for b in range(blocks) for h in range(3)]
    q = [w_ref[h * HALF : (h + 1) * HALF] for h in range(3)]
    w = jnp.concatenate([q[1], q[0], q[2], q[2]], axis=0)
    y = lax.dot_general(x_ref[...], w, NT, preferred_element_type=f32).astype(bf16)
    q_ref[...] = y
    for i in range(2):
        q_scr[i] = y[:, i * LANES : (i + 1) * LANES].astype(f32)

    def rows_of(b):
        return slice(b * SEG0, (b + 1) * SEG0)

    def kv(b, h):
        return kv_ref[rows_of(b), h * LANES : (h + 1) * LANES]

    def ask(b, h):
        keep = jnp.logical_not(low) if acc_low(h) else low
        first = h // 2 * LANES
        q = q_ref[rows_of(b), first : first + LANES]
        return scores(jnp.where(keep, q, jnp.zeros((), bf16)), kv(b, h))

    s = {u: ask(*u) for u in units[:3]}
    am = {}
    for i, u in enumerate(units):
        if i + 3 < len(units):
            s[units[i + 3]] = ask(*units[i + 3])
        b, h = u
        peak, p = soften(s.pop(u), factor)
        am[u] = weigh(p, kv(b, h), h)
        am_scr[h, rows_of(b)] = am[u]
        pk_scr[h, rows_of(b)] = jnp.broadcast_to(peak, am[u].shape)
        if h == 2:
            near_ref[rows_of(b)] = pair(am.pop((b, 0)), am.pop((b, 1)))
    near_ref[rows:] = fold(am_scr[2])
    for copy in copies:
        copy.wait()
    for h in range(3):
        own, own_far = slice(h * per, h * per + mid), slice(h * per + mid, (h + 1) * per)
        mid_rows = pl.ds(mo[h], mid, stride=R1)
        far_rows = pl.ds(fo[h], far, stride=R2)
        am_ref[own], am_ref[own_far] = am_scr[h, mid_rows], am_scr[h, far_rows]
        pk_ref[own], pk_ref[own_far] = pk_scr[h, mid_rows], pk_scr[h, far_rows]
        keep = lane_half((mid, LANES))
        keep = jnp.logical_not(keep) if acc_low(h) else keep
        for at, picked, kept in ((own, mid_rows, keep), (own_far, far_rows, keep[:far])):
            qp_ref[at] = jnp.where(kept, q_scr[h // 2, picked], 0.0).astype(bf16)


def merge_kernel(factor, mid_n, far_n, mo_hbm, fo_hbm, near_ref, qp_ref, am_ref, pk_ref, *rest):
    mids, fars = rest[:mid_n], rest[mid_n : mid_n + far_n]
    attn_ref, mo, fo, attn_scr, am_scr, pk_scr, sems = rest[mid_n + far_n :]
    copies = tell(mo_hbm, fo_hbm, mo, fo, sems)
    rows = near_ref.shape[0] * 2 // 3
    attn_scr[...] = near_ref[...]
    per = qp_ref.shape[0] // 3
    far = per * R1 // (R1 + R2)
    mid = per - far
    heads = range(3)
    own = [slice(h * per, h * per + mid) for h in heads]
    own_far = [slice(h * per + mid, (h + 1) * per) for h in heads]

    def joined(refs, h, whole, at):
        return jnp.concatenate([m[at[h]] if m.shape[0] == 3 * per else m[h] for m in refs], axis=0)

    kv_mid = [joined(mids, h, per, own) for h in heads]
    kv_far = [joined(fars, h, per, own_far) for h in heads]
    s_mid = [scores(qp_ref[own[h]], kv_mid[h]) for h in heads]
    s_far = [scores(qp_ref[own_far[h]], kv_far[h]) for h in heads]
    soft_mid = [soften(s, factor) for s in s_mid]
    soft_far = [soften(s, factor) for s in s_far]
    am_mid = [weigh(soft_mid[h][1], kv_mid[h], h) for h in heads]
    am_far = [weigh(soft_far[h][1], kv_far[h], h) for h in heads]
    out_mid, out_far = [], []
    for h in heads:
        peak_mid = jnp.broadcast_to(soft_mid[h][0], am_mid[h].shape)
        am_scr[h] = am_mid[h]
        pk_scr[h] = peak_mid
        near_peak, near_am = pk_ref[own[h]], am_ref[own[h]]
        top = jnp.maximum(near_peak, peak_mid)
        out_mid.append(
            jnp.exp2((near_peak - top) * factor) * near_am
            + jnp.exp2((peak_mid - top) * factor) * am_mid[h]
        )
    for copy in copies:
        copy.wait()
    for h in heads:
        shared = pl.ds(fo[h] // R1, far, stride=R2 // R1)
        also = fo[h] % R1 == mo[h]
        both_peak = jnp.where(also, pk_scr[h, shared], -1e30)
        both_am = am_scr[h, shared]
        near_peak, near_am = pk_ref[own_far[h]], am_ref[own_far[h]]
        top = jnp.maximum(jnp.maximum(near_peak, both_peak), soft_far[h][0])
        out_far.append(
            jnp.exp2((near_peak - top) * factor) * near_am
            + jnp.exp2((both_peak - top) * factor) * both_am
            + jnp.exp2((soft_far[h][0] - top) * factor) * am_far[h]
        )
    for offset, stride, count, out in ((mo, R1, mid, out_mid), (fo, R2, far, out_far)):
        both = pair(out[0], out[1])
        low = lane_half(both.shape)
        for h, keep in ((0, low), (1, jnp.logical_not(low))):
            at = pl.ds(offset[h], count, stride=stride)
            attn_scr[at] = jnp.where(keep, both, attn_scr[at])
        attn_scr[pl.ds(rows + offset[2], count // 2, stride=stride)] = fold(out[2])
    attn_ref[...] = attn_scr[...].astype(bf16)


def product(first, half, attns, weights):
    total = None
    for attn, weight in zip(attns, weights):
        third = attn[2 * half :]
        if first:
            third = swap(third.astype(f32)).astype(bf16)
        rows = jnp.concatenate([attn[first : first + half], third[:, :HALF]], axis=1)
        part = jnp.dot(rows, weight[...], preferred_element_type=f32)
        total = part if total is None else total + part
    return total


def product_kernel(x_ref, *rest):
    out_ref, count = rest[-1], len(rest) // 2
    half = x_ref.shape[0] // 2
    for first in (0, half):
        at = slice(first, first + half)
        part = product(first, half, rest[:count], rest[count : 2 * count])
        out_ref[at] = x_ref[at].astype(f32) + part


def output_kernel(head_count, place, x_ref, gb_ref, *rest):
    out_ref, resid_scr = rest[-2:]
    count = len(rest) // 2 - 1
    rows, width = x_ref.shape
    half = rows // 2
    cols = width // head_count
    for first in (0, half):
        at = slice(first, first + half)
        resid = x_ref[at].astype(f32) + product(first, half, rest[:count], rest[count : 2 * count])
        mean = jnp.sum(resid, axis=1, keepdims=True) / width
        var = jnp.sum(resid * resid, axis=1, keepdims=True) / width - mean * mean
        resid_scr[at] = (resid - mean) * lax.rsqrt(var + epsilon)
    for i in range(head_count):

        @pl.when(place[0] == i)
        def _():
            mine = resid_scr[:, i * cols : (i + 1) * cols]
            out_ref[...] = (mine * gb_ref[0:1] + gb_ref[1:2]).T.astype(bf16)


IN_VMEM = pl.BlockSpec(memory_space=pltpu.VMEM)
IN_SMEM = pl.BlockSpec(memory_space=pltpu.SMEM)
IN_HBM = pl.BlockSpec(memory_space=pltpu.HBM)


def call(kernel, outs, scratch, scalars, far, near, name, flops, limit):
    return pl.pallas_call(
        kernel,
        out_shape=outs,
        in_specs=[IN_SMEM] * len(scalars) + [IN_HBM] * len(far) + [IN_VMEM] * len(near),
        out_specs=jax.tree.map(lambda _: IN_VMEM, outs),
        scratch_shapes=scratch,
        compiler_params=pltpu.CompilerParams(vmem_limit_bytes=limit << 20),
        name=name,
        cost_estimate=pl.CostEstimate(flops=flops, transcendentals=0, bytes_accessed=4 << 20),
    )(*scalars, *far, *near)


def local(tokens, w_qkv, w_out, gain, bias, mid_offset, far_offset):
    rows, width = tokens.shape
    heads_here = mid_offset.shape[0]
    head_size = width // HEADS
    cols = heads_here * head_size
    factor = math.log2(math.e) / math.sqrt(head_size)
    mid, far = rows // R1, rows // R2
    per = mid + far
    shape = jax.ShapeDtypeStruct
    after = lax.optimization_barrier

    head_count = lax.axis_size("head")
    if head_count & (head_count - 1) == 0:
        paths = [[(i, i ^ r) for i in range(head_count)] for r in range(head_count)]
    else:
        paths = [[(i, (i + r) % head_count) for i in range(head_count)] for r in range(head_count)]

    def to(array, r):
        return lax.ppermute(array, "head", paths[r])

    def spread(array):
        return [array] + [to(array, r) for r in range(1, head_count)]

    two_step = head_count == 4

    def pinned(array):
        return pltpu.with_memory_space_constraint(array, pltpu.HBM)

    w_rows = pinned(jnp.swapaxes(w_qkv, 1, 2))
    offsets = (pinned(mid_offset), pinned(far_offset))
    told = [pltpu.SMEM((heads_here,), jnp.int32)] * 2
    kv, kvp, x, w_query = call(
        project_kernel,
        (
            shape((rows, 3 * LANES), bf16),
            shape((3 * per, LANES), bf16),
            shape((rows, width), bf16),
            shape((cols, width), bf16),
        ),
        [
            *told,
            pltpu.VMEM((2, cols, width), bf16),
            pltpu.VMEM((3, rows, LANES), f32),
            pltpu.SemaphoreType.DMA((7,)),
        ],
        (),
        (*offsets, pinned(tokens), w_rows),
        (),
        "project",
        2 * rows * width * 2 * cols,
        24,
    )

    seq_count = lax.axis_size("seq")
    mid_devs = min(8, seq_count)

    def within(step):
        def partner(i):
            if False:
                return i % mid_devs ^ step
            return (i + step) % mid_devs

        return [(i, i // mid_devs * mid_devs + partner(i)) for i in range(seq_count)]

    if mid_devs == seq_count:
        mids = [kvp] + [lax.ppermute(kvp, "seq", within(s)) for s in range(1, mid_devs)]
        fars = None
    else:
        split = kvp.reshape(3, per, LANES)
        piece = split[:, :mid]
        mids = [piece] + [lax.ppermute(piece, "seq", within(s)) for s in range(1, mid_devs)]
        fars = [lax.all_gather(split[:, mid:], "seq", axis=1, tiled=True)]

    if two_step:
        across = to(w_out, 2)
        beside = to(w_out, 1)
        weights = [w_out, beside, across, to(across, 1)]
    else:
        weights = spread(w_out)

    near, am, pk, qp, gb = call(
        partial(near_kernel, factor),
        (
            shape((rows + rows // 2, LANES), f32),
            shape((3 * per, LANES), f32),
            shape((3 * per, LANES), f32),
            shape((3 * per, LANES), bf16),
            shape((2, cols), f32),
        ),
        [
            *told,
            pltpu.VMEM((3, rows, LANES), f32),
            pltpu.VMEM((3, rows, LANES), f32),
            pltpu.VMEM((2, rows, LANES), f32),
            pltpu.VMEM((rows, 2 * LANES), bf16),
            pltpu.SemaphoreType.DMA((2,)),
        ],
        (),
        offsets,
        (kv, x, w_query, gain.reshape(1, cols), bias.reshape(1, cols)),
        "near",
        1 << 29,
        24,
    )
    attn = call(
        partial(merge_kernel, factor, len(mids), len(fars or mids)),
        shape((rows + rows // 2, LANES), bf16),
        [
            *told,
            pltpu.VMEM((rows + rows // 2, LANES), f32),
            pltpu.VMEM((3, mid, LANES), f32),
            pltpu.VMEM((3, mid, LANES), f32),
            pltpu.SemaphoreType.DMA((2,)),
        ],
        (),
        offsets,
        (near, qp, am, pk, *mids, *(fars or mids)),
        "merge",
        1 << 29,
        24,
    )
    if two_step:
        attn_across = to(attn, 2)
        attns = [attn, to(attn, 1), attn_across, to(attn_across, 1)]
    else:
        attns = spread(attn)

    resid = x
    for r in ((0, 1), (2,)) if two_step else ():
        resid = call(
            product_kernel,
            shape((rows, width), f32),
            [],
            (),
            (),
            (resid, *(attns[i] for i in r), *(weights[i] for i in r)),
            "product",
            len(r) * 2 * rows * cols * width,
            24,
        )
    left = slice(3, None) if two_step else slice(None)
    out = call(
        partial(output_kernel, head_count),
        shape((cols, rows), bf16),
        [pltpu.VMEM((rows, width), f32)],
        (lax.axis_index("head").reshape(1),),
        (),
        (resid, gb, *attns[left], *weights[left]),
        "output",
        2 * rows * width * cols,
        24,
    )
    return out.T


def solution(mesh):
    in_specs = (
        P(("group", "seq"), None),
        P(None, None, "head"),
        P("head", None),
        P("head"),
        P("head"),
        P("head"),
        P("head"),
    )
    out_specs = P(("group", "seq"), "head")
    return jax.shard_map(local, mesh=mesh, in_specs=in_specs, out_specs=out_specs, check_vma=False)
```

```python
from functools import partial
import math

import jax
import jax.numpy as jnp
from jax import lax
from jax.experimental import pallas as pl
from jax.experimental.pallas import tpu as pltpu
from jax.sharding import PartitionSpec as P

HEADS = 12
SEG0 = 128
R1 = 8
R2 = 32
LANES = 128
HALF = 64

epsilon = 1e-05
f32 = jnp.float32
bf16 = jnp.bfloat16

NT = (((1,), (1,)), ((), ()))


def lane_half(shape):
    return lax.broadcasted_iota(jnp.int32, shape, 1) < HALF


def acc_low(head):
    return head % 2 == 0


def project_kernel(
    mo_hbm, fo_hbm, x_ref, w_ref, lanes_ref, kv_ref, kvp_ref, mo, fo, scr, sems
):
    rows = x_ref.shape[0]
    mid, far = rows // R1, rows // R2
    per = mid + far
    half = rows // 2
    copies = tell(mo_hbm, fo_hbm, mo, fo, sems)
    k = [w_ref[1, h * HALF : (h + 1) * HALF] for h in range(3)]
    v = [w_ref[2, h * HALF : (h + 1) * HALF] for h in range(3)]
    w = jnp.concatenate([v[0], k[0], k[1], v[1], v[2], k[2]], axis=0)
    for i in range(2):
        at = slice(i * half, (i + 1) * half)
        y = lax.dot_general(x_ref[at], w, NT, preferred_element_type=f32).astype(bf16)
        kv_ref[at] = y
        for h in range(3):
            scr[h, at] = y[:, h * LANES : (h + 1) * LANES].astype(f32)
    for copy in copies:
        copy.wait()
    for h in range(3):
        mid_rows = pl.ds(mo[h], mid, stride=R1)
        far_rows = pl.ds(fo[h], far, stride=R2)
        kvp_ref[h * per : h * per + mid] = scr[h, mid_rows].astype(bf16)
        kvp_ref[h * per + mid : (h + 1) * per] = scr[h, far_rows].astype(bf16)


def scores(queries, keys_values):
    return lax.dot_general(queries, keys_values, NT, preferred_element_type=f32)


def soften(s, factor):
    peak = jnp.max(s, axis=1, keepdims=True)
    return peak, jnp.exp2((s - peak) * factor).astype(bf16)


def weigh(p, keys_values, head):
    low = lane_half(keys_values.shape)
    is_value = low if acc_low(head) else jnp.logical_not(low)
    values = jnp.where(is_value, keys_values, jnp.ones((), bf16))
    return jnp.dot(p, values, preferred_element_type=f32)


def swap(x):
    return pltpu.roll(x, HALF, 1)


def pair(a, b):
    low = lane_half(a.shape)
    return jnp.where(low, a, b) / swap(jnp.where(low, b, a))


def fold(x):
    half = x.shape[0] // 2
    a, b = x[:half], x[half:]
    low = lane_half(a.shape)
    return jnp.where(low, a, swap(b)) / jnp.where(low, swap(a), b)


def lanes_kernel(out_ref):
    out_ref[...] = lax.broadcasted_iota(jnp.int32, out_ref.shape, 1)


def tell(mo_hbm, fo_hbm, mo, fo, sems):
    copies = [
        pltpu.make_async_copy(mo_hbm, mo, sems.at[0]),
        pltpu.make_async_copy(fo_hbm, fo, sems.at[1]),
    ]
    for copy in copies:
        copy.start()
    return copies


def near_kernel(
    factor,
    mo_hbm,
    fo_hbm,
    kv_ref,
    x_ref,
    w_ref,
    gain_ref,
    bias_ref,
    near_ref,
    am_ref,
    pk_ref,
    qp_ref,
    gb_ref,
    mo,
    fo,
    am_scr,
    pk_scr,
    q_scr,
    q_ref,
    sems,
):
    copies = tell(mo_hbm, fo_hbm, mo, fo, sems)
    gb_ref[0:1] = gain_ref[...]
    gb_ref[1:2] = bias_ref[...]
    rows = kv_ref.shape[0]
    mid, far = rows // R1, rows // R2
    per = mid + far
    low = lane_half((SEG0, LANES))
    blocks = rows // SEG0
    units = [(b, h) for b in range(blocks) for h in range(3)]
    q = [w_ref[0, h * HALF : (h + 1) * HALF] for h in range(3)]
    w = jnp.concatenate([q[1], q[0], q[2], q[2]], axis=0)
    y = lax.dot_general(x_ref[...], w, NT, preferred_element_type=f32).astype(bf16)
    q_ref[...] = y
    for i in range(2):
        q_scr[i] = y[:, i * LANES : (i + 1) * LANES].astype(f32)

    def rows_of(b):
        return slice(b * SEG0, (b + 1) * SEG0)

    def kv(b, h):
        return kv_ref[rows_of(b), h * LANES : (h + 1) * LANES]

    def ask(b, h):
        keep = jnp.logical_not(low) if acc_low(h) else low
        first = h // 2 * LANES
        q = q_ref[rows_of(b), first : first + LANES]
        return scores(jnp.where(keep, q, jnp.zeros((), bf16)), kv(b, h))

    s = {u: ask(*u) for u in units[:3]}
    am = {}
    for i, u in enumerate(units):
        if i + 3 < len(units):
            s[units[i + 3]] = ask(*units[i + 3])
        b, h = u
        peak, p = soften(s.pop(u), factor)
        am[u] = weigh(p, kv(b, h), h)
        am_scr[h, rows_of(b)] = am[u]
        pk_scr[h, rows_of(b)] = jnp.broadcast_to(peak, am[u].shape)
        if h == 2:
            near_ref[rows_of(b)] = pair(am.pop((b, 0)), am.pop((b, 1)))
    near_ref[rows:] = fold(am_scr[2])
    for copy in copies:
        copy.wait()
    for h in range(3):
        own, own_far = slice(h * per, h * per + mid), slice(h * per + mid, (h + 1) * per)
        mid_rows = pl.ds(mo[h], mid, stride=R1)
        far_rows = pl.ds(fo[h], far, stride=R2)
        am_ref[own], am_ref[own_far] = am_scr[h, mid_rows], am_scr[h, far_rows]
        pk_ref[own], pk_ref[own_far] = pk_scr[h, mid_rows], pk_scr[h, far_rows]
        keep = lane_half((mid, LANES))
        keep = jnp.logical_not(keep) if acc_low(h) else keep
        for at, picked, kept in ((own, mid_rows, keep), (own_far, far_rows, keep[:far])):
            qp_ref[at] = jnp.where(kept, q_scr[h // 2, picked], 0.0).astype(bf16)


def merge_kernel(factor, mid_n, far_n, mo_hbm, fo_hbm, near_ref, qp_ref, am_ref, pk_ref, *rest):
    mids, fars = rest[:mid_n], rest[mid_n : mid_n + far_n]
    attn_ref, mo, fo, attn_scr, am_scr, pk_scr, sems = rest[mid_n + far_n :]
    copies = tell(mo_hbm, fo_hbm, mo, fo, sems)
    rows = near_ref.shape[0] * 2 // 3
    attn_scr[...] = near_ref[...]
    per = qp_ref.shape[0] // 3
    far = per * R1 // (R1 + R2)
    mid = per - far
    heads = range(3)
    own = [slice(h * per, h * per + mid) for h in heads]
    own_far = [slice(h * per + mid, (h + 1) * per) for h in heads]

    def joined(refs, h, whole, at):
        return jnp.concatenate([m[at[h]] if m.shape[0] == 3 * per else m[h] for m in refs], axis=0)

    kv_mid = [joined(mids, h, per, own) for h in heads]
    kv_far = [joined(fars, h, per, own_far) for h in heads]
    s_mid = [scores(qp_ref[own[h]], kv_mid[h]) for h in heads]
    s_far = [scores(qp_ref[own_far[h]], kv_far[h]) for h in heads]
    soft_mid = [soften(s, factor) for s in s_mid]
    soft_far = [soften(s, factor) for s in s_far]
    am_mid = [weigh(soft_mid[h][1], kv_mid[h], h) for h in heads]
    am_far = [weigh(soft_far[h][1], kv_far[h], h) for h in heads]
    out_mid, out_far = [], []
    for h in heads:
        peak_mid = jnp.broadcast_to(soft_mid[h][0], am_mid[h].shape)
        am_scr[h] = am_mid[h]
        pk_scr[h] = peak_mid
        near_peak, near_am = pk_ref[own[h]], am_ref[own[h]]
        top = jnp.maximum(near_peak, peak_mid)
        out_mid.append(
            jnp.exp2((near_peak - top) * factor) * near_am
            + jnp.exp2((peak_mid - top) * factor) * am_mid[h]
        )
    for copy in copies:
        copy.wait()
    for h in heads:
        shared = pl.ds(fo[h] // R1, far, stride=R2 // R1)
        also = fo[h] % R1 == mo[h]
        both_peak = jnp.where(also, pk_scr[h, shared], -1e30)
        both_am = am_scr[h, shared]
        near_peak, near_am = pk_ref[own_far[h]], am_ref[own_far[h]]
        top = jnp.maximum(jnp.maximum(near_peak, both_peak), soft_far[h][0])
        out_far.append(
            jnp.exp2((near_peak - top) * factor) * near_am
            + jnp.exp2((both_peak - top) * factor) * both_am
            + jnp.exp2((soft_far[h][0] - top) * factor) * am_far[h]
        )
    for offset, stride, count, out in ((mo, R1, mid, out_mid), (fo, R2, far, out_far)):
        both = pair(out[0], out[1])
        low = lane_half(both.shape)
        for h, keep in ((0, low), (1, jnp.logical_not(low))):
            at = pl.ds(offset[h], count, stride=stride)
            attn_scr[at] = jnp.where(keep, both, attn_scr[at])
        attn_scr[pl.ds(rows + offset[2], count // 2, stride=stride)] = fold(out[2])
    attn_ref[...] = attn_scr[...].astype(bf16)


def product(first, half, attns, weights):
    total = None
    for attn, weight in zip(attns, weights):
        third = attn[2 * half :]
        if first:
            third = swap(third.astype(f32)).astype(bf16)
        rows = jnp.concatenate([attn[first : first + half], third[:, :HALF]], axis=1)
        part = jnp.dot(rows, weight[...], preferred_element_type=f32)
        total = part if total is None else total + part
    return total


def product_kernel(x_ref, *rest):
    out_ref, count = rest[-1], len(rest) // 2
    half = x_ref.shape[0] // 2
    for first in (0, half):
        at = slice(first, first + half)
        part = product(first, half, rest[:count], rest[count : 2 * count])
        out_ref[at] = x_ref[at].astype(f32) + part


def output_kernel(head_count, place, x_ref, gb_ref, *rest):
    out_ref, resid_scr = rest[-2:]
    count = len(rest) // 2 - 1
    rows, width = x_ref.shape
    half = rows // 2
    cols = width // head_count
    for first in (0, half):
        at = slice(first, first + half)
        resid = x_ref[at].astype(f32) + product(first, half, rest[:count], rest[count : 2 * count])
        mean = jnp.sum(resid, axis=1, keepdims=True) / width
        var = jnp.sum(resid * resid, axis=1, keepdims=True) / width - mean * mean
        resid_scr[at] = (resid - mean) * lax.rsqrt(var + epsilon)
    for i in range(head_count):

        @pl.when(place[0] == i)
        def _():
            mine = resid_scr[:, i * cols : (i + 1) * cols]
            out_ref[...] = (mine * gb_ref[0:1] + gb_ref[1:2]).T.astype(bf16)


IN_VMEM = pl.BlockSpec(memory_space=pltpu.VMEM)
IN_SMEM = pl.BlockSpec(memory_space=pltpu.SMEM)
IN_HBM = pl.BlockSpec(memory_space=pltpu.HBM)


def call(kernel, outs, scratch, scalars, far, near, name, flops, limit):
    return pl.pallas_call(
        kernel,
        out_shape=outs,
        in_specs=[IN_SMEM] * len(scalars) + [IN_HBM] * len(far) + [IN_VMEM] * len(near),
        out_specs=jax.tree.map(lambda _: IN_VMEM, outs),
        scratch_shapes=scratch,
        compiler_params=pltpu.CompilerParams(vmem_limit_bytes=limit << 20),
        name=name,
        cost_estimate=pl.CostEstimate(flops=flops, transcendentals=0, bytes_accessed=4 << 20),
    )(*scalars, *far, *near)


def local(tokens, w_qkv, w_out, gain, bias, mid_offset, far_offset):
    rows, width = tokens.shape
    heads_here = mid_offset.shape[0]
    head_size = width // HEADS
    cols = heads_here * head_size
    factor = math.log2(math.e) / math.sqrt(head_size)
    mid, far = rows // R1, rows // R2
    per = mid + far
    shape = jax.ShapeDtypeStruct
    after = lax.optimization_barrier

    head_count = lax.axis_size("head")
    if head_count & (head_count - 1) == 0:
        paths = [[(i, i ^ r) for i in range(head_count)] for r in range(head_count)]
    else:
        paths = [[(i, (i + r) % head_count) for i in range(head_count)] for r in range(head_count)]

    def to(array, r):
        return lax.ppermute(array, "head", paths[r])

    def spread(array):
        return [array] + [to(array, r) for r in range(1, head_count)]

    two_step = head_count == 4

    def pinned(array):
        return pltpu.with_memory_space_constraint(array, pltpu.HBM)

    x = pltpu.with_memory_space_constraint(tokens, pltpu.VMEM)
    w_rows = pltpu.with_memory_space_constraint(jnp.swapaxes(w_qkv, 1, 2), pltpu.VMEM)
    lanes = call(
        lanes_kernel, shape((8, LANES), jnp.int32), [], (), (), (), "lanes", 460 << 20, 24
    )
    offsets = (pinned(mid_offset), pinned(far_offset))
    told = [pltpu.SMEM((heads_here,), jnp.int32)] * 2
    kv, kvp = call(
        project_kernel,
        (
            shape((rows, 3 * LANES), bf16),
            shape((3 * per, LANES), bf16),
        ),
        [
            *told,
            pltpu.VMEM((3, rows, LANES), f32),
            pltpu.SemaphoreType.DMA((2,)),
        ],
        (),
        offsets,
        (x, w_rows, lanes),
        "project",
        2 * rows * width * 2 * cols,
        24,
    )

    seq_count = lax.axis_size("seq")
    mid_devs = min(8, seq_count)

    def within(step):
        def partner(i):
            if False:
                return i % mid_devs ^ step
            return (i + step) % mid_devs

        return [(i, i // mid_devs * mid_devs + partner(i)) for i in range(seq_count)]

    if mid_devs == seq_count:
        mids = [kvp] + [lax.ppermute(kvp, "seq", within(s)) for s in range(1, mid_devs)]
        fars = None
    else:
        split = kvp.reshape(3, per, LANES)
        piece = split[:, :mid]
        mids = [piece] + [lax.ppermute(piece, "seq", within(s)) for s in range(1, mid_devs)]
        fars = [lax.all_gather(split[:, mid:], "seq", axis=1, tiled=True)]

    if two_step:
        across = to(after((w_out, lanes))[0], 2)
        beside = to(w_out, 1)
        weights = [w_out, beside, across, to(across, 1)]
    else:
        weights = spread(w_out)

    near, am, pk, qp, gb = call(
        partial(near_kernel, factor),
        (
            shape((rows + rows // 2, LANES), f32),
            shape((3 * per, LANES), f32),
            shape((3 * per, LANES), f32),
            shape((3 * per, LANES), bf16),
            shape((2, cols), f32),
        ),
        [
            *told,
            pltpu.VMEM((3, rows, LANES), f32),
            pltpu.VMEM((3, rows, LANES), f32),
            pltpu.VMEM((2, rows, LANES), f32),
            pltpu.VMEM((rows, 2 * LANES), bf16),
            pltpu.SemaphoreType.DMA((2,)),
        ],
        (),
        offsets,
        (kv, x, w_rows, gain.reshape(1, cols), bias.reshape(1, cols)),
        "near",
        1 << 29,
        24,
    )
    attn = call(
        partial(merge_kernel, factor, len(mids), len(fars or mids)),
        shape((rows + rows // 2, LANES), bf16),
        [
            *told,
            pltpu.VMEM((rows + rows // 2, LANES), f32),
            pltpu.VMEM((3, mid, LANES), f32),
            pltpu.VMEM((3, mid, LANES), f32),
            pltpu.SemaphoreType.DMA((2,)),
        ],
        (),
        offsets,
        (near, qp, am, pk, *mids, *(fars or mids)),
        "merge",
        1 << 29,
        24,
    )
    if two_step:
        attn_across = to(attn, 2)
        attns = [attn, to(attn, 1), attn_across, to(attn_across, 1)]
    else:
        attns = spread(attn)

    resid = x
    for r in ((0, 1), (2,)) if two_step else ():
        resid = call(
            product_kernel,
            shape((rows, width), f32),
            [],
            (),
            (),
            (resid, *(attns[i] for i in r), *(weights[i] for i in r)),
            "product",
            len(r) * 2 * rows * cols * width,
            24,
        )
    left = slice(3, None) if two_step else slice(None)
    out = call(
        partial(output_kernel, head_count),
        shape((cols, rows), bf16),
        [pltpu.VMEM((rows, width), f32)],
        (lax.axis_index("head").reshape(1),),
        (),
        (resid, gb, *attns[left], *weights[left]),
        "output",
        2 * rows * width * cols,
        24,
    )
    return out.T


def solution(mesh):
    in_specs = (
        P(("group", "seq"), None),
        P(None, None, "head"),
        P("head", None),
        P("head"),
        P("head"),
        P("head"),
        P("head"),
    )
    out_specs = P(("group", "seq"), "head")
    return jax.shard_map(local, mesh=mesh, in_specs=in_specs, out_specs=out_specs, check_vma=False)
```

```python
from functools import partial
import math

import jax
import jax.numpy as jnp
from jax import lax
from jax.experimental import pallas as pl
from jax.experimental.pallas import tpu as pltpu
from jax.sharding import PartitionSpec as P

HEADS = 12
SEG0 = 128
R1 = 8
R2 = 32
LANES = 128
HALF = 64

epsilon = 1e-05
f32 = jnp.float32
bf16 = jnp.bfloat16

NT = (((1,), (1,)), ((), ()))


def lane_half(shape):
    return lax.broadcasted_iota(jnp.int32, shape, 1) < HALF


def acc_low(head):
    return head % 2 == 0


def project_kernel(
    mo_from, fo_from, x_ref, w_ref, lanes_ref, kv_ref, kvp_ref, mo, fo, scr, sems
):
    rows = x_ref.shape[0]
    mid, far = rows // R1, rows // R2
    per = mid + far
    half = rows // 2
    copies = tell(mo_from, fo_from, mo, fo, sems)
    k = [w_ref[1, h * HALF : (h + 1) * HALF] for h in range(3)]
    v = [w_ref[2, h * HALF : (h + 1) * HALF] for h in range(3)]
    w = jnp.concatenate([v[0], k[0], k[1], v[1], v[2], k[2]], axis=0)
    for i in range(2):
        at = slice(i * half, (i + 1) * half)
        y = lax.dot_general(x_ref[at], w, NT, preferred_element_type=f32).astype(bf16)
        kv_ref[at] = y
        for h in range(3):
            scr[h, at] = y[:, h * LANES : (h + 1) * LANES].astype(f32)
    for copy in copies:
        copy.wait()
    for h in range(3):
        mid_rows = pl.ds(mo[h], mid, stride=R1)
        far_rows = pl.ds(fo[h], far, stride=R2)
        kvp_ref[h * per : h * per + mid] = scr[h, mid_rows].astype(bf16)
        kvp_ref[h * per + mid : (h + 1) * per] = scr[h, far_rows].astype(bf16)


def scores(queries, keys_values):
    return lax.dot_general(queries, keys_values, NT, preferred_element_type=f32)


def soften(s, factor):
    peak = jnp.max(s, axis=1, keepdims=True)
    return peak, jnp.exp2((s - peak) * factor).astype(bf16)


def weigh(p, keys_values, head):
    low = lane_half(keys_values.shape)
    is_value = low if acc_low(head) else jnp.logical_not(low)
    values = jnp.where(is_value, keys_values, jnp.ones((), bf16))
    return jnp.dot(p, values, preferred_element_type=f32)


def swap(x):
    return pltpu.roll(x, HALF, 1)


def pair(a, b):
    low = lane_half(a.shape)
    return jnp.where(low, a, b) / swap(jnp.where(low, b, a))


def fold(x):
    half = x.shape[0] // 2
    a, b = x[:half], x[half:]
    low = lane_half(a.shape)
    return jnp.where(low, a, swap(b)) / jnp.where(low, swap(a), b)


def lanes_kernel(out_ref):
    out_ref[...] = lax.broadcasted_iota(jnp.int32, out_ref.shape, 1)


def tell(mo_from, fo_from, mo, fo, sems):
    copies = [
        pltpu.make_async_copy(mo_from, mo, sems.at[0]),
        pltpu.make_async_copy(fo_from, fo, sems.at[1]),
    ]
    for copy in copies:
        copy.start()
    return copies


def near_kernel(
    factor,
    mo_from,
    fo_from,
    kv_ref,
    x_ref,
    w_ref,
    gain_ref,
    bias_ref,
    near_ref,
    am_ref,
    pk_ref,
    qp_ref,
    gb_ref,
    mo,
    fo,
    am_scr,
    pk_scr,
    q_scr,
    q_ref,
    sems,
):
    copies = tell(mo_from, fo_from, mo, fo, sems)
    gb_ref[0:1] = gain_ref[...]
    gb_ref[1:2] = bias_ref[...]
    rows = kv_ref.shape[0]
    mid, far = rows // R1, rows // R2
    per = mid + far
    low = lane_half((SEG0, LANES))
    blocks = rows // SEG0
    units = [(b, h) for b in range(blocks) for h in range(3)]
    q = [w_ref[0, h * HALF : (h + 1) * HALF] for h in range(3)]
    w = jnp.concatenate([q[1], q[0], q[2], q[2]], axis=0)
    y = lax.dot_general(x_ref[...], w, NT, preferred_element_type=f32).astype(bf16)
    q_ref[...] = y
    for i in range(2):
        q_scr[i] = y[:, i * LANES : (i + 1) * LANES].astype(f32)

    def rows_of(b):
        return slice(b * SEG0, (b + 1) * SEG0)

    def kv(b, h):
        return kv_ref[rows_of(b), h * LANES : (h + 1) * LANES]

    def ask(b, h):
        keep = jnp.logical_not(low) if acc_low(h) else low
        first = h // 2 * LANES
        q = q_ref[rows_of(b), first : first + LANES]
        return scores(jnp.where(keep, q, jnp.zeros((), bf16)), kv(b, h))

    s = {u: ask(*u) for u in units[:3]}
    am = {}
    for i, u in enumerate(units):
        if i + 3 < len(units):
            s[units[i + 3]] = ask(*units[i + 3])
        b, h = u
        peak, p = soften(s.pop(u), factor)
        am[u] = weigh(p, kv(b, h), h)
        am_scr[h, rows_of(b)] = am[u]
        pk_scr[h, rows_of(b)] = jnp.broadcast_to(peak, am[u].shape)
        if h == 2:
            near_ref[rows_of(b)] = pair(am.pop((b, 0)), am.pop((b, 1)))
    near_ref[rows:] = fold(am_scr[2])
    for copy in copies:
        copy.wait()
    for h in range(3):
        own, own_far = slice(h * per, h * per + mid), slice(h * per + mid, (h + 1) * per)
        mid_rows = pl.ds(mo[h], mid, stride=R1)
        far_rows = pl.ds(fo[h], far, stride=R2)
        am_ref[own], am_ref[own_far] = am_scr[h, mid_rows], am_scr[h, far_rows]
        pk_ref[own], pk_ref[own_far] = pk_scr[h, mid_rows], pk_scr[h, far_rows]
        keep = lane_half((mid, LANES))
        keep = jnp.logical_not(keep) if acc_low(h) else keep
        for at, picked, kept in ((own, mid_rows, keep), (own_far, far_rows, keep[:far])):
            qp_ref[at] = jnp.where(kept, q_scr[h // 2, picked], 0.0).astype(bf16)


def merge_kernel(factor, mid_n, far_n, mo_from, fo_from, near_ref, qp_ref, am_ref, pk_ref, *rest):
    mids, fars = rest[:mid_n], rest[mid_n : mid_n + far_n]
    attn_ref, mo, fo, attn_scr, am_scr, pk_scr, sems = rest[mid_n + far_n :]
    copies = tell(mo_from, fo_from, mo, fo, sems)
    rows = near_ref.shape[0] * 2 // 3
    attn_scr[...] = near_ref[...]
    per = qp_ref.shape[0] // 3
    far = per * R1 // (R1 + R2)
    mid = per - far
    heads = range(3)
    own = [slice(h * per, h * per + mid) for h in heads]
    own_far = [slice(h * per + mid, (h + 1) * per) for h in heads]

    def joined(refs, h, whole, at):
        return jnp.concatenate([m[at[h]] if m.shape[0] == 3 * per else m[h] for m in refs], axis=0)

    kv_mid = [joined(mids, h, per, own) for h in heads]
    kv_far = [joined(fars, h, per, own_far) for h in heads]
    s_mid = [scores(qp_ref[own[h]], kv_mid[h]) for h in heads]
    s_far = [scores(qp_ref[own_far[h]], kv_far[h]) for h in heads]
    soft_mid = [soften(s, factor) for s in s_mid]
    soft_far = [soften(s, factor) for s in s_far]
    am_mid = [weigh(soft_mid[h][1], kv_mid[h], h) for h in heads]
    am_far = [weigh(soft_far[h][1], kv_far[h], h) for h in heads]
    out_mid, out_far = [], []
    for h in heads:
        peak_mid = jnp.broadcast_to(soft_mid[h][0], am_mid[h].shape)
        am_scr[h] = am_mid[h]
        pk_scr[h] = peak_mid
        near_peak, near_am = pk_ref[own[h]], am_ref[own[h]]
        top = jnp.maximum(near_peak, peak_mid)
        out_mid.append(
            jnp.exp2((near_peak - top) * factor) * near_am
            + jnp.exp2((peak_mid - top) * factor) * am_mid[h]
        )
    for copy in copies:
        copy.wait()
    for h in heads:
        shared = pl.ds(fo[h] // R1, far, stride=R2 // R1)
        also = fo[h] % R1 == mo[h]
        both_peak = jnp.where(also, pk_scr[h, shared], -1e30)
        both_am = am_scr[h, shared]
        near_peak, near_am = pk_ref[own_far[h]], am_ref[own_far[h]]
        top = jnp.maximum(jnp.maximum(near_peak, both_peak), soft_far[h][0])
        out_far.append(
            jnp.exp2((near_peak - top) * factor) * near_am
            + jnp.exp2((both_peak - top) * factor) * both_am
            + jnp.exp2((soft_far[h][0] - top) * factor) * am_far[h]
        )
    for offset, stride, count, out in ((mo, R1, mid, out_mid), (fo, R2, far, out_far)):
        both = pair(out[0], out[1])
        low = lane_half(both.shape)
        for h, keep in ((0, low), (1, jnp.logical_not(low))):
            at = pl.ds(offset[h], count, stride=stride)
            attn_scr[at] = jnp.where(keep, both, attn_scr[at])
        attn_scr[pl.ds(rows + offset[2], count // 2, stride=stride)] = fold(out[2])
    attn_ref[...] = attn_scr[...].astype(bf16)


def product(first, half, attns, weights):
    total = None
    for attn, weight in zip(attns, weights):
        third = attn[2 * half :]
        if first:
            third = swap(third.astype(f32)).astype(bf16)
        rows = jnp.concatenate([attn[first : first + half], third[:, :HALF]], axis=1)
        part = jnp.dot(rows, weight[...], preferred_element_type=f32)
        total = part if total is None else total + part
    return total


def product_kernel(x_ref, *rest):
    out_ref, count = rest[-1], len(rest) // 2
    half = x_ref.shape[0] // 2
    for first in (0, half):
        at = slice(first, first + half)
        part = product(first, half, rest[:count], rest[count : 2 * count])
        out_ref[at] = x_ref[at].astype(f32) + part


def own_kernel(place, x_ref, attn_ref, w_ref, last_ref, out_ref, own_ref, last_own_ref):
    product_kernel(x_ref, attn_ref, w_ref, out_ref)
    cols = own_ref.shape[1]
    for i in range(out_ref.shape[1] // cols):

        @pl.when(place[0] == i)
        def _():
            at = slice(i * cols, (i + 1) * cols)
            own_ref[...] = out_ref[:, at]
            last_own_ref[...] = last_ref[:, at]


def output_kernel(x_ref, own_ref, last_own_ref, gb_ref, attn_ref, w_ref, out_hbm, out_ref, sems):
    copies = []
    rows, width = x_ref.shape
    step = rows // 4
    for i in range(4):
        at = slice(i * step, (i + 1) * step)
        third = attn_ref[rows + i % 2 * step : rows + (i % 2 + 1) * step]
        if i > 1:
            third = swap(third.astype(f32)).astype(bf16)
        attn = jnp.concatenate([attn_ref[at], third[:, :HALF]], axis=1)
        resid = x_ref[at] + jnp.dot(attn, w_ref[...], preferred_element_type=f32)
        mean = jnp.sum(resid, axis=1, keepdims=True) / width
        var = jnp.sum(resid * resid, axis=1, keepdims=True) / width - mean * mean
        mine = own_ref[at] + jnp.dot(attn, last_own_ref[...], preferred_element_type=f32)
        normed = (mine - mean) * lax.rsqrt(var + epsilon) * gb_ref[0:1] + gb_ref[1:2]
        out_ref[:, at] = normed.astype(bf16).T
        copies.append(pltpu.make_async_copy(out_ref.at[:, at], out_hbm.at[:, at], sems.at[i]))
        copies[i].start()
    for copy in copies:
        copy.wait()


IN_VMEM = pl.BlockSpec(memory_space=pltpu.VMEM)
IN_SMEM = pl.BlockSpec(memory_space=pltpu.SMEM)
IN_HBM = pl.BlockSpec(memory_space=pltpu.HBM)


def call(kernel, outs, scratch, scalars, far, near, name, flops, limit, held=None):
    return pl.pallas_call(
        kernel,
        out_shape=outs,
        in_specs=[IN_SMEM] * len(scalars) + [IN_HBM] * len(far) + [IN_VMEM] * len(near),
        out_specs=jax.tree.map(lambda _: held or IN_VMEM, outs),
        scratch_shapes=scratch,
        compiler_params=pltpu.CompilerParams(vmem_limit_bytes=limit << 20),
        name=name,
        cost_estimate=pl.CostEstimate(flops=flops, transcendentals=0, bytes_accessed=4 << 20),
    )(*scalars, *far, *near)


def local(tokens, w_qkv, w_out, gain, bias, mid_offset, far_offset):
    rows, width = tokens.shape
    heads_here = mid_offset.shape[0]
    head_size = width // HEADS
    cols = heads_here * head_size
    factor = math.log2(math.e) / math.sqrt(head_size)
    mid, far = rows // R1, rows // R2
    per = mid + far
    shape = jax.ShapeDtypeStruct
    after = lax.optimization_barrier

    head_count = lax.axis_size("head")
    if head_count & (head_count - 1) == 0:
        paths = [[(i, i ^ r) for i in range(head_count)] for r in range(head_count)]
    else:
        paths = [[(i, (i + r) % head_count) for i in range(head_count)] for r in range(head_count)]

    def to(array, r):
        return lax.ppermute(array, "head", paths[r])

    def spread(array):
        return [array] + [to(array, r) for r in range(1, head_count)]

    two_step = head_count == 4

    def pinned(array):
        return pltpu.with_memory_space_constraint(array, pltpu.HBM)

    x = pltpu.with_memory_space_constraint(tokens, pltpu.VMEM)
    w_rows = pltpu.with_memory_space_constraint(jnp.swapaxes(w_qkv, 1, 2), pltpu.VMEM)
    lanes = call(
        lanes_kernel, shape((8, LANES), jnp.int32), [], (), (), (), "lanes", 460 << 20, 24
    )
    offsets = (pinned(mid_offset), pinned(far_offset))
    told = [pltpu.SMEM((heads_here,), jnp.int32)] * 2
    kv, kvp = call(
        project_kernel,
        (
            shape((rows, 3 * LANES), bf16),
            shape((3 * per, LANES), bf16),
        ),
        [
            *told,
            pltpu.VMEM((3, rows, LANES), f32),
            pltpu.SemaphoreType.DMA((2,)),
        ],
        (),
        (),
        (mid_offset, far_offset, x, w_rows, lanes),
        "project",
        2 * rows * width * 2 * cols,
        24,
    )

    seq_count = lax.axis_size("seq")
    mid_devs = min(8, seq_count)

    def within(step):
        return [
            (i, i // mid_devs * mid_devs + (i + step) % mid_devs) for i in range(seq_count)
        ]

    if mid_devs == seq_count:
        mids = [kvp] + [lax.ppermute(kvp, "seq", within(s)) for s in range(1, mid_devs)]
        fars = None
    else:
        split = kvp.reshape(3, per, LANES)
        piece = split[:, :mid]
        mids = [piece] + [lax.ppermute(piece, "seq", within(s)) for s in range(1, mid_devs)]
        fars = [lax.all_gather(split[:, mid:], "seq", axis=1, tiled=True)]

    if two_step:
        across = to(after((w_out, lanes))[0], 2)
        beside = to(w_out, 1)
        weights = [w_out, beside, across, to(across, 1)]
    else:
        weights = spread(w_out)

    near, am, pk, qp, gb = call(
        partial(near_kernel, factor),
        (
            shape((rows + rows // 2, LANES), f32),
            shape((3 * per, LANES), f32),
            shape((3 * per, LANES), f32),
            shape((3 * per, LANES), bf16),
            shape((2, cols), f32),
        ),
        [
            *told,
            pltpu.VMEM((3, rows, LANES), f32),
            pltpu.VMEM((3, rows, LANES), f32),
            pltpu.VMEM((2, rows, LANES), f32),
            pltpu.VMEM((rows, 2 * LANES), bf16),
            pltpu.SemaphoreType.DMA((2,)),
        ],
        (),
        offsets,
        (kv, x, w_rows, gain.reshape(1, cols), bias.reshape(1, cols)),
        "near",
        1 << 29,
        24,
    )
    attn = call(
        partial(merge_kernel, factor, len(mids), len(fars or mids)),
        shape((rows + rows // 2, LANES), bf16),
        [
            *told,
            pltpu.VMEM((rows + rows // 2, LANES), f32),
            pltpu.VMEM((3, mid, LANES), f32),
            pltpu.VMEM((3, mid, LANES), f32),
            pltpu.SemaphoreType.DMA((2,)),
        ],
        (),
        (),
        (mid_offset, far_offset, near, qp, am, pk, *mids, *(fars or mids)),
        "merge",
        1 << 29,
        24,
    )
    if two_step:
        attn_across = to(attn, 2)
        attns = [attn, to(attn, 1), attn_across, to(attn_across, 1)]
    else:
        attns = spread(attn)

    flops = 2 * rows * cols * width
    resid = call(
        product_kernel,
        shape((rows, width), f32),
        [],
        (),
        (),
        (x, *attns[:-2], *weights[:-2]),
        "product",
        (head_count - 2) * flops,
        24,
    )
    resid, own, last_own = call(
        own_kernel,
        (
            shape((rows, width), f32),
            shape((rows, cols), f32),
            shape((cols, cols), bf16),
        ),
        [],
        (lax.axis_index("head").reshape(1),),
        (),
        (resid, attns[-2], *weights[-2:]),
        "own",
        flops,
        24,
    )
    out = call(
        output_kernel,
        shape((cols, rows), bf16),
        [pltpu.VMEM((cols, rows), bf16), pltpu.SemaphoreType.DMA((4,))],
        (),
        (),
        (resid, own, last_own, gb, attns[-1], weights[-1]),
        "output",
        flops,
        24,
        IN_HBM,
    )
    return out.T


def solution(mesh):
    in_specs = (
        P(("group", "seq"), None),
        P(None, None, "head"),
        P("head", None),
        P("head"),
        P("head"),
        P("head"),
        P("head"),
    )
    out_specs = P(("group", "seq"), "head")
    return jax.shard_map(local, mesh=mesh, in_specs=in_specs, out_specs=out_specs, check_vma=False)
```

```python
from functools import partial
import math

import jax
import jax.numpy as jnp
from jax import lax
from jax.experimental import pallas as pl
from jax.experimental.pallas import tpu as pltpu
from jax.sharding import PartitionSpec as P

HEADS = 12
SEG0 = 128
R1 = 8
R2 = 32
LANES = 128
HALF = 64

epsilon = 1e-05
f32 = jnp.float32
bf16 = jnp.bfloat16

NT = (((1,), (1,)), ((), ()))


def lane_half(shape):
    return lax.broadcasted_iota(jnp.int32, shape, 1) < HALF


def acc_low(head):
    return head % 2 == 0


def project_kernel(
    mo_from, fo_from, x_ref, w_ref, lanes_ref, kv_ref, kvp_ref, mo, fo, scr, sems
):
    rows = x_ref.shape[0]
    mid, far = rows // R1, rows // R2
    per = mid + far
    half = rows // 2
    copies = tell(mo_from, fo_from, mo, fo, sems)
    k = [w_ref[1, h * HALF : (h + 1) * HALF] for h in range(3)]
    v = [w_ref[2, h * HALF : (h + 1) * HALF] for h in range(3)]
    w = jnp.concatenate([v[0], k[0], k[1], v[1], v[2], k[2]], axis=0)
    for i in range(2):
        at = slice(i * half, (i + 1) * half)
        y = lax.dot_general(x_ref[at], w, NT, preferred_element_type=f32).astype(bf16)
        kv_ref[at] = y
        for h in range(3):
            scr[h, at] = y[:, h * LANES : (h + 1) * LANES].astype(f32)
    for copy in copies:
        copy.wait()
    for h in range(3):
        mid_rows = pl.ds(mo[h], mid, stride=R1)
        far_rows = pl.ds(fo[h], far, stride=R2)
        kvp_ref[h * per : h * per + mid] = scr[h, mid_rows].astype(bf16)
        kvp_ref[h * per + mid : (h + 1) * per] = scr[h, far_rows].astype(bf16)


def scores(queries, keys_values):
    return lax.dot_general(queries, keys_values, NT, preferred_element_type=f32)


def soften(s, factor):
    peak = jnp.max(s, axis=1, keepdims=True)
    return peak, jnp.exp2((s - peak) * factor).astype(bf16)


def weigh(p, keys_values, head):
    low = lane_half(keys_values.shape)
    is_value = low if acc_low(head) else jnp.logical_not(low)
    values = jnp.where(is_value, keys_values, jnp.ones((), bf16))
    return jnp.dot(p, values, preferred_element_type=f32)


def swap(x):
    return pltpu.roll(x, HALF, 1)


def pair(a, b):
    low = lane_half(a.shape)
    return jnp.where(low, a, b) / swap(jnp.where(low, b, a))


def fold(x):
    half = x.shape[0] // 2
    a, b = x[:half], x[half:]
    low = lane_half(a.shape)
    return jnp.where(low, a, swap(b)) / jnp.where(low, swap(a), b)


def lanes_kernel(out_ref):
    out_ref[...] = lax.broadcasted_iota(jnp.int32, out_ref.shape, 1)


def tell(mo_from, fo_from, mo, fo, sems):
    copies = [
        pltpu.make_async_copy(mo_from, mo, sems.at[0]),
        pltpu.make_async_copy(fo_from, fo, sems.at[1]),
    ]
    for copy in copies:
        copy.start()
    return copies


def near_kernel(
    factor,
    mo_from,
    fo_from,
    kv_ref,
    x_ref,
    w_ref,
    gain_ref,
    bias_ref,
    near_ref,
    am_ref,
    pk_ref,
    qp_ref,
    gb_ref,
    mo,
    fo,
    am_scr,
    pk_scr,
    q_scr,
    q_ref,
    sems,
):
    copies = tell(mo_from, fo_from, mo, fo, sems)
    gb_ref[0:1] = gain_ref[...]
    gb_ref[1:2] = bias_ref[...]
    rows = kv_ref.shape[0]
    mid, far = rows // R1, rows // R2
    per = mid + far
    low = lane_half((SEG0, LANES))
    blocks = rows // SEG0
    units = [(b, h) for b in range(blocks) for h in range(3)]
    q = [w_ref[0, h * HALF : (h + 1) * HALF] for h in range(3)]
    w = jnp.concatenate([q[1], q[0], q[2], q[2]], axis=0)
    y = lax.dot_general(x_ref[...], w, NT, preferred_element_type=f32).astype(bf16)
    q_ref[...] = y
    for i in range(2):
        q_scr[i] = y[:, i * LANES : (i + 1) * LANES].astype(f32)

    def rows_of(b):
        return slice(b * SEG0, (b + 1) * SEG0)

    def kv(b, h):
        return kv_ref[rows_of(b), h * LANES : (h + 1) * LANES]

    def ask(b, h):
        keep = jnp.logical_not(low) if acc_low(h) else low
        first = h // 2 * LANES
        q = q_ref[rows_of(b), first : first + LANES]
        return scores(jnp.where(keep, q, jnp.zeros((), bf16)), kv(b, h))

    s = {u: ask(*u) for u in units[:3]}
    am = {}
    for i, u in enumerate(units):
        if i + 3 < len(units):
            s[units[i + 3]] = ask(*units[i + 3])
        b, h = u
        peak, p = soften(s.pop(u), factor)
        am[u] = weigh(p, kv(b, h), h)
        am_scr[h, rows_of(b)] = am[u]
        pk_scr[h, rows_of(b)] = jnp.broadcast_to(peak, am[u].shape)
        if h == 2:
            near_ref[rows_of(b)] = pair(am.pop((b, 0)), am.pop((b, 1)))
    near_ref[rows:] = fold(am_scr[2])
    for copy in copies:
        copy.wait()
    for h in range(3):
        own, own_far = slice(h * per, h * per + mid), slice(h * per + mid, (h + 1) * per)
        mid_rows = pl.ds(mo[h], mid, stride=R1)
        far_rows = pl.ds(fo[h], far, stride=R2)
        am_ref[own], am_ref[own_far] = am_scr[h, mid_rows], am_scr[h, far_rows]
        pk_ref[own], pk_ref[own_far] = pk_scr[h, mid_rows], pk_scr[h, far_rows]
        keep = lane_half((mid, LANES))
        keep = jnp.logical_not(keep) if acc_low(h) else keep
        for at, picked, kept in ((own, mid_rows, keep), (own_far, far_rows, keep[:far])):
            qp_ref[at] = jnp.where(kept, q_scr[h // 2, picked], 0.0).astype(bf16)


def merge_kernel(factor, mid_n, far_n, mo_from, fo_from, near_ref, qp_ref, am_ref, pk_ref, *rest):
    mids, fars = rest[:mid_n], rest[mid_n : mid_n + far_n]
    attn_ref, mo, fo, attn_scr, am_scr, pk_scr, sems = rest[mid_n + far_n :]
    copies = tell(mo_from, fo_from, mo, fo, sems)
    rows = near_ref.shape[0] * 2 // 3
    attn_scr[...] = near_ref[...]
    per = qp_ref.shape[0] // 3
    far = per * R1 // (R1 + R2)
    mid = per - far
    heads = range(3)
    own = [slice(h * per, h * per + mid) for h in heads]
    own_far = [slice(h * per + mid, (h + 1) * per) for h in heads]

    def joined(refs, h, whole, at):
        return jnp.concatenate([m[at[h]] if m.shape[0] == 3 * per else m[h] for m in refs], axis=0)

    kv_mid = [joined(mids, h, per, own) for h in heads]
    kv_far = [joined(fars, h, per, own_far) for h in heads]
    s_mid = [scores(qp_ref[own[h]], kv_mid[h]) for h in heads]
    s_far = [scores(qp_ref[own_far[h]], kv_far[h]) for h in heads]
    soft_mid = [soften(s, factor) for s in s_mid]
    soft_far = [soften(s, factor) for s in s_far]
    am_mid = [weigh(soft_mid[h][1], kv_mid[h], h) for h in heads]
    am_far = [weigh(soft_far[h][1], kv_far[h], h) for h in heads]
    out_mid, out_far = [], []
    for h in heads:
        peak_mid = jnp.broadcast_to(soft_mid[h][0], am_mid[h].shape)
        am_scr[h] = am_mid[h]
        pk_scr[h] = peak_mid
        near_peak, near_am = pk_ref[own[h]], am_ref[own[h]]
        top = jnp.maximum(near_peak, peak_mid)
        out_mid.append(
            jnp.exp2((near_peak - top) * factor) * near_am
            + jnp.exp2((peak_mid - top) * factor) * am_mid[h]
        )
    for copy in copies:
        copy.wait()
    for h in heads:
        shared = pl.ds(fo[h] // R1, far, stride=R2 // R1)
        also = fo[h] % R1 == mo[h]
        both_peak = jnp.where(also, pk_scr[h, shared], -1e30)
        both_am = am_scr[h, shared]
        near_peak, near_am = pk_ref[own_far[h]], am_ref[own_far[h]]
        top = jnp.maximum(jnp.maximum(near_peak, both_peak), soft_far[h][0])
        out_far.append(
            jnp.exp2((near_peak - top) * factor) * near_am
            + jnp.exp2((both_peak - top) * factor) * both_am
            + jnp.exp2((soft_far[h][0] - top) * factor) * am_far[h]
        )
    for offset, stride, count, out in ((mo, R1, mid, out_mid), (fo, R2, far, out_far)):
        both = pair(out[0], out[1])
        low = lane_half(both.shape)
        for h, keep in ((0, low), (1, jnp.logical_not(low))):
            at = pl.ds(offset[h], count, stride=stride)
            attn_scr[at] = jnp.where(keep, both, attn_scr[at])
        attn_scr[pl.ds(rows + offset[2], count // 2, stride=stride)] = fold(out[2])
    attn_ref[...] = attn_scr[...].astype(bf16)


def product(first, half, attns, weights):
    total = None
    for attn, weight in zip(attns, weights):
        third = attn[2 * half :]
        if first:
            third = swap(third.astype(f32)).astype(bf16)
        rows = jnp.concatenate([attn[first : first + half], third[:, :HALF]], axis=1)
        part = jnp.dot(rows, weight[...], preferred_element_type=f32)
        total = part if total is None else total + part
    return total


def product_kernel(x_ref, *rest):
    out_ref, count = rest[-1], len(rest) // 2
    half = x_ref.shape[0] // 2
    for first in (0, half):
        at = slice(first, first + half)
        part = product(first, half, rest[:count], rest[count : 2 * count])
        out_ref[at] = x_ref[at].astype(f32) + part


def own_kernel(place, last_ref, *refs):
    out_ref, own_ref, last_own_ref = refs[-3:]
    product_kernel(*refs[:-3], out_ref)
    cols = own_ref.shape[1]
    for i in range(out_ref.shape[1] // cols):

        @pl.when(place[0] == i)
        def _():
            at = slice(i * cols, (i + 1) * cols)
            own_ref[...] = out_ref[:, at]
            last_own_ref[...] = last_ref[:, at]


def output_kernel(x_ref, own_ref, last_own_ref, gb_ref, attn_ref, w_ref, out_hbm, out_ref, sems):
    copies = []
    rows, width = x_ref.shape
    step = rows // 4
    for i in range(4):
        at = slice(i * step, (i + 1) * step)
        third = attn_ref[rows + i % 2 * step : rows + (i % 2 + 1) * step]
        if i > 1:
            third = swap(third.astype(f32)).astype(bf16)
        attn = jnp.concatenate([attn_ref[at], third[:, :HALF]], axis=1)
        resid = x_ref[at] + jnp.dot(attn, w_ref[...], preferred_element_type=f32)
        tiles = [resid[:, j : j + LANES] for j in range(0, width, LANES)]
        mean = jnp.sum(sum(tiles), axis=1, keepdims=True) / width
        var = jnp.sum(sum(t * t for t in tiles), axis=1, keepdims=True) / width - mean * mean
        mine = own_ref[at] + jnp.dot(attn, last_own_ref[...], preferred_element_type=f32)
        normed = (mine - mean) * lax.rsqrt(var + epsilon) * gb_ref[0:1] + gb_ref[1:2]
        out_ref[:, at] = normed.astype(bf16).T
        copies.append(pltpu.make_async_copy(out_ref.at[:, at], out_hbm.at[:, at], sems.at[i]))
        copies[i].start()
    for copy in copies:
        copy.wait()


IN_VMEM = pl.BlockSpec(memory_space=pltpu.VMEM)
IN_SMEM = pl.BlockSpec(memory_space=pltpu.SMEM)
IN_HBM = pl.BlockSpec(memory_space=pltpu.HBM)


def call(kernel, outs, scratch, scalars, far, near, name, flops, limit, held=None):
    return pl.pallas_call(
        kernel,
        out_shape=outs,
        in_specs=[IN_SMEM] * len(scalars) + [IN_HBM] * len(far) + [IN_VMEM] * len(near),
        out_specs=jax.tree.map(lambda _: held or IN_VMEM, outs),
        scratch_shapes=scratch,
        compiler_params=pltpu.CompilerParams(vmem_limit_bytes=limit << 20),
        name=name,
        cost_estimate=pl.CostEstimate(flops=flops, transcendentals=0, bytes_accessed=4 << 20),
    )(*scalars, *far, *near)


def local(tokens, w_qkv, w_out, gain, bias, mid_offset, far_offset):
    rows, width = tokens.shape
    heads_here = mid_offset.shape[0]
    head_size = width // HEADS
    cols = heads_here * head_size
    factor = math.log2(math.e) / math.sqrt(head_size)
    mid, far = rows // R1, rows // R2
    per = mid + far
    shape = jax.ShapeDtypeStruct
    after = lax.optimization_barrier

    head_count = lax.axis_size("head")
    if head_count & (head_count - 1) == 0:
        paths = [[(i, i ^ r) for i in range(head_count)] for r in range(head_count)]
    else:
        paths = [[(i, (i + r) % head_count) for i in range(head_count)] for r in range(head_count)]

    def to(array, r):
        return lax.ppermute(array, "head", paths[r])

    def spread(array):
        return [array] + [to(array, r) for r in range(1, head_count)]

    two_step = head_count == 4

    def pinned(array):
        return pltpu.with_memory_space_constraint(array, pltpu.HBM)

    x = pltpu.with_memory_space_constraint(tokens, pltpu.VMEM)
    w_rows = pltpu.with_memory_space_constraint(jnp.swapaxes(w_qkv, 1, 2), pltpu.VMEM)
    lanes = call(
        lanes_kernel, shape((8, LANES), jnp.int32), [], (), (), (), "lanes", 460 << 20, 24
    )
    offsets = (pinned(mid_offset), pinned(far_offset))
    told = [pltpu.SMEM((heads_here,), jnp.int32)] * 2
    kv, kvp = call(
        project_kernel,
        (
            shape((rows, 3 * LANES), bf16),
            shape((3 * per, LANES), bf16),
        ),
        [
            *told,
            pltpu.VMEM((3, rows, LANES), f32),
            pltpu.SemaphoreType.DMA((2,)),
        ],
        (),
        (),
        (mid_offset, far_offset, x, w_rows, lanes),
        "project",
        2 * rows * width * 2 * cols,
        24,
    )

    seq_count = lax.axis_size("seq")
    mid_devs = min(8, seq_count)

    def within(step):
        return [
            (i, i // mid_devs * mid_devs + (i + step) % mid_devs) for i in range(seq_count)
        ]

    if mid_devs == seq_count:
        mids = [kvp] + [lax.ppermute(kvp, "seq", within(s)) for s in range(1, mid_devs)]
        fars = None
    else:
        split = kvp.reshape(3, per, LANES)
        piece = split[:, :mid]
        mids = [piece] + [lax.ppermute(piece, "seq", within(s)) for s in range(1, mid_devs)]
        fars = [lax.all_gather(split[:, mid:], "seq", axis=1, tiled=True)]

    if two_step:
        across = to(after((w_out, lanes))[0], 2)
        beside = to(w_out, 1)
        weights = [w_out, beside, across, to(across, 1)]
    else:
        weights = spread(w_out)

    near, am, pk, qp, gb = call(
        partial(near_kernel, factor),
        (
            shape((rows + rows // 2, LANES), f32),
            shape((3 * per, LANES), f32),
            shape((3 * per, LANES), f32),
            shape((3 * per, LANES), bf16),
            shape((2, cols), f32),
        ),
        [
            *told,
            pltpu.VMEM((3, rows, LANES), f32),
            pltpu.VMEM((3, rows, LANES), f32),
            pltpu.VMEM((2, rows, LANES), f32),
            pltpu.VMEM((rows, 2 * LANES), bf16),
            pltpu.SemaphoreType.DMA((2,)),
        ],
        (),
        offsets,
        (kv, x, w_rows, gain.reshape(1, cols), bias.reshape(1, cols)),
        "near",
        1 << 29,
        24,
    )
    attn = call(
        partial(merge_kernel, factor, len(mids), len(fars or mids)),
        shape((rows + rows // 2, LANES), bf16),
        [
            *told,
            pltpu.VMEM((rows + rows // 2, LANES), f32),
            pltpu.VMEM((3, mid, LANES), f32),
            pltpu.VMEM((3, mid, LANES), f32),
            pltpu.SemaphoreType.DMA((2,)),
        ],
        (),
        (),
        (mid_offset, far_offset, near, qp, am, pk, *mids, *(fars or mids)),
        "merge",
        1 << 29,
        24,
    )
    if two_step:
        attn_across = to(attn, 2)
        attns = [attn, to(attn, 1), attn_across, to(attn_across, 1)]
    else:
        attns = spread(attn)

    flops = 2 * rows * cols * width
    resid, own, last_own = call(
        own_kernel,
        (
            shape((rows, width), f32),
            shape((rows, cols), f32),
            shape((cols, cols), bf16),
        ),
        [],
        (lax.axis_index("head").reshape(1),),
        (),
        (weights[-1], x, *attns[:-1], *weights[:-1]),
        "own",
        (head_count - 1) * flops,
        24,
    )
    out = call(
        output_kernel,
        shape((cols, rows), bf16),
        [pltpu.VMEM((cols, rows), bf16), pltpu.SemaphoreType.DMA((4,))],
        (),
        (),
        (resid, own, last_own, gb, attns[-1], weights[-1]),
        "output",
        flops,
        24,
        IN_HBM,
    )
    return out.T


def solution(mesh):
    in_specs = (
        P(("group", "seq"), None),
        P(None, None, "head"),
        P("head", None),
        P("head"),
        P("head"),
        P("head"),
        P("head"),
    )
    out_specs = P(("group", "seq"), "head")
    return jax.shard_map(local, mesh=mesh, in_specs=in_specs, out_specs=out_specs, check_vma=False)
```

```python
from functools import partial
import math

import jax
import jax.numpy as jnp
from jax import lax
from jax.experimental import pallas as pl
from jax.experimental.pallas import tpu as pltpu
from jax.sharding import PartitionSpec as P

HEADS = 12
SEG0 = 128
R1 = 8
R2 = 32
LANES = 128
HALF = 64

epsilon = 1e-05
f32 = jnp.float32
bf16 = jnp.bfloat16

NT = (((1,), (1,)), ((), ()))


def lane_half(shape):
    return lax.broadcasted_iota(jnp.int32, shape, 1) < HALF


def acc_low(head):
    return head % 2 == 0


def project_kernel(
    mo_from, fo_from, x_ref, w_ref, lanes_ref, kv_ref, kvp_ref, mo, fo, scr, sems
):
    rows = x_ref.shape[0]
    mid, far = rows // R1, rows // R2
    per = mid + far
    half = rows // 2
    copies = tell(mo_from, fo_from, mo, fo, sems)
    k = [w_ref[1, h * HALF : (h + 1) * HALF] for h in range(3)]
    v = [w_ref[2, h * HALF : (h + 1) * HALF] for h in range(3)]
    w = jnp.concatenate([v[0], k[0], k[1], v[1], v[2], k[2]], axis=0)
    for i in range(2):
        at = slice(i * half, (i + 1) * half)
        y = lax.dot_general(x_ref[at], w, NT, preferred_element_type=f32).astype(bf16)
        kv_ref[at] = y
        for h in range(3):
            scr[h, at] = y[:, h * LANES : (h + 1) * LANES].astype(f32)
    for copy in copies:
        copy.wait()
    for h in range(3):
        mid_rows = pl.ds(mo[h], mid, stride=R1)
        far_rows = pl.ds(fo[h], far, stride=R2)
        kvp_ref[h * per : h * per + mid] = scr[h, mid_rows].astype(bf16)
        kvp_ref[h * per + mid : (h + 1) * per] = scr[h, far_rows].astype(bf16)


def scores(queries, keys_values):
    return lax.dot_general(queries, keys_values, NT, preferred_element_type=f32)


def soften(s, factor):
    peak = jnp.max(s, axis=1, keepdims=True)
    return peak, jnp.exp2((s - peak) * factor).astype(bf16)


def weigh(p, keys_values, head):
    low = lane_half(keys_values.shape)
    is_value = low if acc_low(head) else jnp.logical_not(low)
    values = jnp.where(is_value, keys_values, jnp.ones((), bf16))
    return jnp.dot(p, values, preferred_element_type=f32)


def swap(x):
    return pltpu.roll(x, HALF, 1)


def pair(a, b):
    low = lane_half(a.shape)
    return jnp.where(low, a, b) / swap(jnp.where(low, b, a))


def fold(x):
    half = x.shape[0] // 2
    a, b = x[:half], x[half:]
    low = lane_half(a.shape)
    return jnp.where(low, a, swap(b)) / jnp.where(low, swap(a), b)


def lanes_kernel(out_ref):
    out_ref[...] = lax.broadcasted_iota(jnp.int32, out_ref.shape, 1)


def tell(mo_from, fo_from, mo, fo, sems):
    copies = [
        pltpu.make_async_copy(mo_from, mo, sems.at[0]),
        pltpu.make_async_copy(fo_from, fo, sems.at[1]),
    ]
    for copy in copies:
        copy.start()
    return copies


def near_kernel(
    factor,
    mo_from,
    fo_from,
    kv_ref,
    x_ref,
    w_ref,
    gain_ref,
    bias_ref,
    near_ref,
    am_ref,
    pk_ref,
    qp_ref,
    gb_ref,
    mo,
    fo,
    am_scr,
    pk_scr,
    q_scr,
    q_ref,
    sems,
):
    copies = tell(mo_from, fo_from, mo, fo, sems)
    gb_ref[0:1] = gain_ref[...]
    gb_ref[1:2] = bias_ref[...]
    rows = kv_ref.shape[0]
    mid, far = rows // R1, rows // R2
    per = mid + far
    low = lane_half((SEG0, LANES))
    blocks = rows // SEG0
    units = [(b, h) for b in range(blocks) for h in range(3)]
    q = [w_ref[0, h * HALF : (h + 1) * HALF] for h in range(3)]
    w = jnp.concatenate([q[1], q[0], q[2], q[2]], axis=0)
    y = lax.dot_general(x_ref[...], w, NT, preferred_element_type=f32).astype(bf16)
    q_ref[...] = y
    for i in range(2):
        q_scr[i] = y[:, i * LANES : (i + 1) * LANES].astype(f32)

    def rows_of(b):
        return slice(b * SEG0, (b + 1) * SEG0)

    def kv(b, h):
        return kv_ref[rows_of(b), h * LANES : (h + 1) * LANES]

    def ask(b, h):
        keep = jnp.logical_not(low) if acc_low(h) else low
        first = h // 2 * LANES
        q = q_ref[rows_of(b), first : first + LANES]
        return scores(jnp.where(keep, q, jnp.zeros((), bf16)), kv(b, h))

    s = {u: ask(*u) for u in units[:3]}
    am = {}
    for i, u in enumerate(units):
        if i + 3 < len(units):
            s[units[i + 3]] = ask(*units[i + 3])
        b, h = u
        peak, p = soften(s.pop(u), factor)
        am[u] = weigh(p, kv(b, h), h)
        am_scr[h, rows_of(b)] = am[u]
        pk_scr[h, rows_of(b)] = jnp.broadcast_to(peak, am[u].shape)
        if h == 2:
            near_ref[rows_of(b)] = pair(am.pop((b, 0)), am.pop((b, 1)))
    near_ref[rows:] = fold(am_scr[2])
    for copy in copies:
        copy.wait()
    for h in range(3):
        own, own_far = slice(h * per, h * per + mid), slice(h * per + mid, (h + 1) * per)
        mid_rows = pl.ds(mo[h], mid, stride=R1)
        far_rows = pl.ds(fo[h], far, stride=R2)
        am_ref[own], am_ref[own_far] = am_scr[h, mid_rows], am_scr[h, far_rows]
        pk_ref[own], pk_ref[own_far] = pk_scr[h, mid_rows], pk_scr[h, far_rows]
        keep = lane_half((mid, LANES))
        keep = jnp.logical_not(keep) if acc_low(h) else keep
        for at, picked, kept in ((own, mid_rows, keep), (own_far, far_rows, keep[:far])):
            qp_ref[at] = jnp.where(kept, q_scr[h // 2, picked], 0.0).astype(bf16)


def merge_kernel(factor, mid_n, far_n, mo_from, fo_from, near_ref, qp_ref, am_ref, pk_ref, *rest):
    mids, fars = rest[:mid_n], rest[mid_n : mid_n + far_n]
    attn_ref, mo, fo, attn_scr, am_scr, pk_scr, sems = rest[mid_n + far_n :]
    copies = tell(mo_from, fo_from, mo, fo, sems)
    rows = near_ref.shape[0] * 2 // 3
    attn_scr[...] = near_ref[...]
    per = qp_ref.shape[0] // 3
    far = per * R1 // (R1 + R2)
    mid = per - far
    heads = range(3)
    own = [slice(h * per, h * per + mid) for h in heads]
    own_far = [slice(h * per + mid, (h + 1) * per) for h in heads]

    def joined(refs, h, whole, at):
        return jnp.concatenate([m[at[h]] if m.shape[0] == 3 * per else m[h] for m in refs], axis=0)

    kv_mid = [joined(mids, h, per, own) for h in heads]
    kv_far = [joined(fars, h, per, own_far) for h in heads]
    s_mid = [scores(qp_ref[own[h]], kv_mid[h]) for h in heads]
    s_far = [scores(qp_ref[own_far[h]], kv_far[h]) for h in heads]
    soft_mid = [soften(s, factor) for s in s_mid]
    soft_far = [soften(s, factor) for s in s_far]
    am_mid = [weigh(soft_mid[h][1], kv_mid[h], h) for h in heads]
    am_far = [weigh(soft_far[h][1], kv_far[h], h) for h in heads]
    out_mid, out_far = [], []
    for h in heads:
        peak_mid = jnp.broadcast_to(soft_mid[h][0], am_mid[h].shape)
        am_scr[h] = am_mid[h]
        pk_scr[h] = peak_mid
        near_peak, near_am = pk_ref[own[h]], am_ref[own[h]]
        top = jnp.maximum(near_peak, peak_mid)
        out_mid.append(
            jnp.exp2((near_peak - top) * factor) * near_am
            + jnp.exp2((peak_mid - top) * factor) * am_mid[h]
        )
    for copy in copies:
        copy.wait()
    for h in heads:
        shared = pl.ds(fo[h] // R1, far, stride=R2 // R1)
        also = fo[h] % R1 == mo[h]
        both_peak = jnp.where(also, pk_scr[h, shared], -1e30)
        both_am = am_scr[h, shared]
        near_peak, near_am = pk_ref[own_far[h]], am_ref[own_far[h]]
        top = jnp.maximum(jnp.maximum(near_peak, both_peak), soft_far[h][0])
        out_far.append(
            jnp.exp2((near_peak - top) * factor) * near_am
            + jnp.exp2((both_peak - top) * factor) * both_am
            + jnp.exp2((soft_far[h][0] - top) * factor) * am_far[h]
        )
    for offset, stride, count, out in ((mo, R1, mid, out_mid), (fo, R2, far, out_far)):
        both = pair(out[0], out[1])
        low = lane_half(both.shape)
        for h, keep in ((0, low), (1, jnp.logical_not(low))):
            at = pl.ds(offset[h], count, stride=stride)
            attn_scr[at] = jnp.where(keep, both, attn_scr[at])
        attn_scr[pl.ds(rows + offset[2], count // 2, stride=stride)] = fold(out[2])
    attn_ref[...] = attn_scr[...].astype(bf16)


def product(first, half, attns, weights):
    total = None
    for attn, weight in zip(attns, weights):
        third = attn[2 * half :]
        if first:
            third = swap(third.astype(f32)).astype(bf16)
        rows = jnp.concatenate([attn[first : first + half], third[:, :HALF]], axis=1)
        part = jnp.dot(rows, weight[...], preferred_element_type=f32)
        total = part if total is None else total + part
    return total


def product_kernel(x_ref, *rest):
    out_ref, count = rest[-1], len(rest) // 2
    half = x_ref.shape[0] // 2
    for first in (0, half):
        at = slice(first, first + half)
        part = product(first, half, rest[:count], rest[count : 2 * count])
        out_ref[at] = x_ref[at].astype(f32) + part


def own_kernel(place, x_ref, attn_ref, w_ref, last_ref, out_ref, own_ref, last_own_ref):
    product_kernel(x_ref, attn_ref, w_ref, out_ref)
    cols = own_ref.shape[1]
    for i in range(out_ref.shape[1] // cols):

        @pl.when(place[0] == i)
        def _():
            at = slice(i * cols, (i + 1) * cols)
            own_ref[...] = out_ref[:, at]
            last_own_ref[...] = last_ref[:, at]


def output_kernel(x_ref, own_ref, last_own_ref, gb_ref, attn_ref, w_ref, out_hbm, out_ref, sems):
    copies = []
    rows, width = x_ref.shape
    step = rows // 4
    for i in range(4):
        at = slice(i * step, (i + 1) * step)
        third = attn_ref[rows + i % 2 * step : rows + (i % 2 + 1) * step]
        if i > 1:
            third = swap(third.astype(f32)).astype(bf16)
        attn = jnp.concatenate([attn_ref[at], third[:, :HALF]], axis=1)
        resid = x_ref[at] + jnp.dot(attn, w_ref[...], preferred_element_type=f32)
        tiles = [resid[:, j : j + LANES] for j in range(0, width, LANES)]
        mean = jnp.sum(sum(tiles), axis=1, keepdims=True) / width
        var = jnp.sum(sum(t * t for t in tiles), axis=1, keepdims=True) / width - mean * mean
        mine = own_ref[at] + jnp.dot(attn, last_own_ref[...], preferred_element_type=f32)
        normed = (mine - mean) * lax.rsqrt(var + epsilon) * gb_ref[0:1] + gb_ref[1:2]
        out_ref[:, at] = normed.astype(bf16).T
        copies.append(pltpu.make_async_copy(out_ref.at[:, at], out_hbm.at[:, at], sems.at[i]))
        copies[i].start()
    for copy in copies:
        copy.wait()


IN_VMEM = pl.BlockSpec(memory_space=pltpu.VMEM)
IN_SMEM = pl.BlockSpec(memory_space=pltpu.SMEM)
IN_HBM = pl.BlockSpec(memory_space=pltpu.HBM)


def call(kernel, outs, scratch, scalars, far, near, name, flops, limit, held=None):
    return pl.pallas_call(
        kernel,
        out_shape=outs,
        in_specs=[IN_SMEM] * len(scalars) + [IN_HBM] * len(far) + [IN_VMEM] * len(near),
        out_specs=jax.tree.map(lambda _: held or IN_VMEM, outs),
        scratch_shapes=scratch,
        compiler_params=pltpu.CompilerParams(vmem_limit_bytes=limit << 20),
        name=name,
        cost_estimate=pl.CostEstimate(flops=flops, transcendentals=0, bytes_accessed=4 << 20),
    )(*scalars, *far, *near)


def local(tokens, w_qkv, w_out, gain, bias, mid_offset, far_offset):
    rows, width = tokens.shape
    heads_here = mid_offset.shape[0]
    head_size = width // HEADS
    cols = heads_here * head_size
    factor = math.log2(math.e) / math.sqrt(head_size)
    mid, far = rows // R1, rows // R2
    per = mid + far
    shape = jax.ShapeDtypeStruct
    after = lax.optimization_barrier

    head_count = lax.axis_size("head")
    if head_count & (head_count - 1) == 0:
        paths = [[(i, i ^ r) for i in range(head_count)] for r in range(head_count)]
    else:
        paths = [[(i, (i + r) % head_count) for i in range(head_count)] for r in range(head_count)]

    def to(array, r):
        return lax.ppermute(array, "head", paths[r])

    def spread(array):
        return [array] + [to(array, r) for r in range(1, head_count)]

    two_step = head_count == 4

    def pinned(array):
        return pltpu.with_memory_space_constraint(array, pltpu.HBM)

    x = pltpu.with_memory_space_constraint(tokens, pltpu.VMEM)
    w_rows = pltpu.with_memory_space_constraint(jnp.swapaxes(w_qkv, 1, 2), pltpu.VMEM)
    lanes = call(
        lanes_kernel, shape((8, LANES), jnp.int32), [], (), (), (), "lanes", 460 << 20, 24
    )
    offsets = (pinned(mid_offset), pinned(far_offset))
    told = [pltpu.SMEM((heads_here,), jnp.int32)] * 2
    kv, kvp = call(
        project_kernel,
        (
            shape((rows, 3 * LANES), bf16),
            shape((3 * per, LANES), bf16),
        ),
        [
            *told,
            pltpu.VMEM((3, rows, LANES), f32),
            pltpu.SemaphoreType.DMA((2,)),
        ],
        (),
        (),
        (mid_offset, far_offset, x, w_rows, lanes),
        "project",
        2 * rows * width * 2 * cols,
        24,
    )

    seq_count = lax.axis_size("seq")
    mid_devs = min(8, seq_count)

    def within(step):
        return [
            (i, i // mid_devs * mid_devs + (i + step) % mid_devs) for i in range(seq_count)
        ]

    if mid_devs == seq_count:
        mids = [kvp] + [lax.ppermute(kvp, "seq", within(s)) for s in range(1, mid_devs)]
        fars = None
    else:
        split = kvp.reshape(3, per, LANES)
        piece = split[:, :mid]
        mids = [piece] + [lax.ppermute(piece, "seq", within(s)) for s in range(1, mid_devs)]
        fars = [lax.all_gather(split[:, mid:], "seq", axis=1, tiled=True)]

    if two_step:
        across = to(after((w_out, lanes))[0], 2)
        beside = to(w_out, 1)
        weights = [w_out, beside, across, to(across, 1)]
    else:
        weights = spread(w_out)

    near, am, pk, qp, gb = call(
        partial(near_kernel, factor),
        (
            shape((rows + rows // 2, LANES), f32),
            shape((3 * per, LANES), f32),
            shape((3 * per, LANES), f32),
            shape((3 * per, LANES), bf16),
            shape((2, cols), f32),
        ),
        [
            *told,
            pltpu.VMEM((3, rows, LANES), f32),
            pltpu.VMEM((3, rows, LANES), f32),
            pltpu.VMEM((2, rows, LANES), f32),
            pltpu.VMEM((rows, 2 * LANES), bf16),
            pltpu.SemaphoreType.DMA((2,)),
        ],
        (),
        offsets,
        (kv, x, w_rows, gain.reshape(1, cols), bias.reshape(1, cols)),
        "near",
        1 << 29,
        24,
    )
    attn = call(
        partial(merge_kernel, factor, len(mids), len(fars or mids)),
        shape((rows + rows // 2, LANES), bf16),
        [
            *told,
            pltpu.VMEM((rows + rows // 2, LANES), f32),
            pltpu.VMEM((3, mid, LANES), f32),
            pltpu.VMEM((3, mid, LANES), f32),
            pltpu.SemaphoreType.DMA((2,)),
        ],
        (),
        (),
        (mid_offset, far_offset, near, qp, am, pk, *mids, *(fars or mids)),
        "merge",
        1 << 29,
        24,
    )
    if two_step:
        attn_across = to(attn, 2)
        attns = [attn, to(attn, 1), attn_across, to(attn_across, 1)]
    else:
        attns = spread(attn)

    flops = 2 * rows * cols * width
    resid = call(
        product_kernel,
        shape((rows, width), f32),
        [],
        (),
        (),
        (x, *attns[:-2], *weights[:-2]),
        "product",
        (head_count - 2) * flops,
        24,
    )
    resid, own, last_own = call(
        own_kernel,
        (
            shape((rows, width), f32),
            shape((rows, cols), f32),
            shape((cols, cols), bf16),
        ),
        [],
        (lax.axis_index("head").reshape(1),),
        (),
        (resid, attns[-2], *weights[-2:]),
        "own",
        flops,
        24,
    )
    out = call(
        output_kernel,
        shape((cols, rows), bf16),
        [pltpu.VMEM((cols, rows), bf16), pltpu.SemaphoreType.DMA((4,))],
        (),
        (),
        (resid, own, last_own, gb, attns[-1], weights[-1]),
        "output",
        flops,
        24,
        IN_HBM,
    )
    return out.T


def solution(mesh):
    in_specs = (
        P(("group", "seq"), None),
        P(None, None, "head"),
        P("head", None),
        P("head"),
        P("head"),
        P("head"),
        P("head"),
    )
    out_specs = P(("group", "seq"), "head")
    return jax.shard_map(local, mesh=mesh, in_specs=in_specs, out_specs=out_specs, check_vma=False)
```

```python
from functools import partial
import math

import jax
import jax.numpy as jnp
from jax import lax
from jax.experimental import pallas as pl
from jax.experimental.pallas import tpu as pltpu
from jax.sharding import PartitionSpec as P

HEADS = 12
SEG0 = 128
R1 = 8
R2 = 32
LANES = 128
HALF = 64

epsilon = 1e-05
f32 = jnp.float32
bf16 = jnp.bfloat16

NT = (((1,), (1,)), ((), ()))


def lane_half(shape):
    return lax.broadcasted_iota(jnp.int32, shape, 1) < HALF


def acc_low(head):
    return head % 2 == 0


def project_kernel(
    mo_from, fo_from, x_ref, w_ref, lanes_ref, kv_ref, kvp_ref, mo, fo, scr, sems
):
    rows = x_ref.shape[0]
    mid, far = rows // R1, rows // R2
    per = mid + far
    half = rows // 2
    copies = tell(mo_from, fo_from, mo, fo, sems)
    k = [w_ref[1, h * HALF : (h + 1) * HALF] for h in range(3)]
    v = [w_ref[2, h * HALF : (h + 1) * HALF] for h in range(3)]
    w = jnp.concatenate([v[0], k[0], k[1], v[1], v[2], k[2]], axis=0)
    for i in range(2):
        at = slice(i * half, (i + 1) * half)
        y = lax.dot_general(x_ref[at], w, NT, preferred_element_type=f32).astype(bf16)
        kv_ref[at] = y
        for h in range(3):
            scr[h, at] = y[:, h * LANES : (h + 1) * LANES].astype(f32)
    for copy in copies:
        copy.wait()
    for h in range(3):
        mid_rows = pl.ds(mo[h], mid, stride=R1)
        far_rows = pl.ds(fo[h], far, stride=R2)
        kvp_ref[h * per : h * per + mid] = scr[h, mid_rows].astype(bf16)
        kvp_ref[h * per + mid : (h + 1) * per] = scr[h, far_rows].astype(bf16)


def scores(queries, keys_values):
    return lax.dot_general(queries, keys_values, NT, preferred_element_type=f32)


def soften(s, factor):
    peak = jnp.max(s, axis=1, keepdims=True)
    return peak, jnp.exp2((s - peak) * factor).astype(bf16)


def weigh(p, keys_values, head):
    low = lane_half(keys_values.shape)
    is_value = low if acc_low(head) else jnp.logical_not(low)
    values = jnp.where(is_value, keys_values, jnp.ones((), bf16))
    return jnp.dot(p, values, preferred_element_type=f32)


def swap(x):
    return pltpu.roll(x, HALF, 1)


def pair(a, b):
    low = lane_half(a.shape)
    return jnp.where(low, a, b) / swap(jnp.where(low, b, a))


def fold(x):
    half = x.shape[0] // 2
    a, b = x[:half], x[half:]
    low = lane_half(a.shape)
    return jnp.where(low, a, swap(b)) / jnp.where(low, swap(a), b)


def lanes_kernel(out_ref):
    out_ref[...] = lax.broadcasted_iota(jnp.int32, out_ref.shape, 1)


def tell(mo_from, fo_from, mo, fo, sems):
    copies = [
        pltpu.make_async_copy(mo_from, mo, sems.at[0]),
        pltpu.make_async_copy(fo_from, fo, sems.at[1]),
    ]
    for copy in copies:
        copy.start()
    return copies


def near_kernel(
    factor,
    mo_from,
    fo_from,
    kv_ref,
    x_ref,
    w_ref,
    gain_ref,
    bias_ref,
    near_ref,
    am_ref,
    pk_ref,
    qp_ref,
    gb_ref,
    mo,
    fo,
    am_scr,
    pk_scr,
    q_scr,
    q_ref,
    sems,
):
    copies = tell(mo_from, fo_from, mo, fo, sems)
    gb_ref[0:1] = gain_ref[...]
    gb_ref[1:2] = bias_ref[...]
    rows = kv_ref.shape[0]
    mid, far = rows // R1, rows // R2
    per = mid + far
    low = lane_half((SEG0, LANES))
    blocks = rows // SEG0
    units = [(b, h) for b in range(blocks) for h in range(3)]
    q = [w_ref[0, h * HALF : (h + 1) * HALF] for h in range(3)]
    w = jnp.concatenate([q[1], q[0], q[2], q[2]], axis=0)
    y = lax.dot_general(x_ref[...], w, NT, preferred_element_type=f32).astype(bf16)
    q_ref[...] = y
    for i in range(2):
        q_scr[i] = y[:, i * LANES : (i + 1) * LANES].astype(f32)

    def rows_of(b):
        return slice(b * SEG0, (b + 1) * SEG0)

    def kv(b, h):
        return kv_ref[rows_of(b), h * LANES : (h + 1) * LANES]

    def ask(b, h):
        keep = jnp.logical_not(low) if acc_low(h) else low
        first = h // 2 * LANES
        q = q_ref[rows_of(b), first : first + LANES]
        return scores(jnp.where(keep, q, jnp.zeros((), bf16)), kv(b, h))

    s = {u: ask(*u) for u in units[:3]}
    am = {}
    for i, u in enumerate(units):
        if i + 3 < len(units):
            s[units[i + 3]] = ask(*units[i + 3])
        b, h = u
        peak, p = soften(s.pop(u), factor)
        am[u] = weigh(p, kv(b, h), h)
        am_scr[h, rows_of(b)] = am[u]
        pk_scr[h, rows_of(b)] = jnp.broadcast_to(peak, am[u].shape)
        if h == 2:
            near_ref[rows_of(b)] = pair(am.pop((b, 0)), am.pop((b, 1)))
    near_ref[rows:] = fold(am_scr[2])
    for copy in copies:
        copy.wait()
    for h in range(3):
        own, own_far = slice(h * per, h * per + mid), slice(h * per + mid, (h + 1) * per)
        mid_rows = pl.ds(mo[h], mid, stride=R1)
        far_rows = pl.ds(fo[h], far, stride=R2)
        am_ref[own], am_ref[own_far] = am_scr[h, mid_rows], am_scr[h, far_rows]
        pk_ref[own], pk_ref[own_far] = pk_scr[h, mid_rows], pk_scr[h, far_rows]
        keep = lane_half((mid, LANES))
        keep = jnp.logical_not(keep) if acc_low(h) else keep
        for at, picked, kept in ((own, mid_rows, keep), (own_far, far_rows, keep[:far])):
            qp_ref[at] = jnp.where(kept, q_scr[h // 2, picked], 0.0).astype(bf16)


def merge_kernel(factor, mid_n, far_n, mo_from, fo_from, near_ref, qp_ref, am_ref, pk_ref, *rest):
    mids, fars = rest[:mid_n], rest[mid_n : mid_n + far_n]
    attn_ref, mo, fo, attn_scr, am_scr, pk_scr, sems = rest[mid_n + far_n :]
    copies = tell(mo_from, fo_from, mo, fo, sems)
    rows = near_ref.shape[0] * 2 // 3
    attn_scr[...] = near_ref[...]
    per = qp_ref.shape[0] // 3
    far = per * R1 // (R1 + R2)
    mid = per - far
    heads = range(3)
    own = [slice(h * per, h * per + mid) for h in heads]
    own_far = [slice(h * per + mid, (h + 1) * per) for h in heads]

    def joined(refs, h, whole, at):
        return jnp.concatenate([m[at[h]] if m.shape[0] == 3 * per else m[h] for m in refs], axis=0)

    kv_mid = [joined(mids, h, per, own) for h in heads]
    kv_far = [joined(fars, h, per, own_far) for h in heads]
    s_mid = [scores(qp_ref[own[h]], kv_mid[h]) for h in heads]
    s_far = [scores(qp_ref[own_far[h]], kv_far[h]) for h in heads]
    soft_mid = [soften(s, factor) for s in s_mid]
    soft_far = [soften(s, factor) for s in s_far]
    am_mid = [weigh(soft_mid[h][1], kv_mid[h], h) for h in heads]
    am_far = [weigh(soft_far[h][1], kv_far[h], h) for h in heads]
    for copy in copies:
        copy.wait()
    out_mid, out_far = [], []
    for h in heads:
        peak_mid = jnp.broadcast_to(soft_mid[h][0], am_mid[h].shape)
        am_scr[h] = am_mid[h]
        pk_scr[h] = peak_mid
        near_peak, near_am = pk_ref[own[h]], am_ref[own[h]]
        top = jnp.maximum(near_peak, peak_mid)
        out_mid.append(
            jnp.exp2((near_peak - top) * factor) * near_am
            + jnp.exp2((peak_mid - top) * factor) * am_mid[h]
        )
    for h in heads:
        shared = pl.ds(fo[h] // R1, far, stride=R2 // R1)
        also = fo[h] % R1 == mo[h]
        both_peak = jnp.where(also, pk_scr[h, shared], -1e30)
        both_am = am_scr[h, shared]
        near_peak, near_am = pk_ref[own_far[h]], am_ref[own_far[h]]
        top = jnp.maximum(jnp.maximum(near_peak, both_peak), soft_far[h][0])
        out_far.append(
            jnp.exp2((near_peak - top) * factor) * near_am
            + jnp.exp2((both_peak - top) * factor) * both_am
            + jnp.exp2((soft_far[h][0] - top) * factor) * am_far[h]
        )
    for offset, stride, count, out in ((mo, R1, mid, out_mid), (fo, R2, far, out_far)):
        both = pair(out[0], out[1])
        low = lane_half(both.shape)
        for h, keep in ((0, low), (1, jnp.logical_not(low))):
            at = pl.ds(offset[h], count, stride=stride)
            attn_scr[at] = jnp.where(keep, both, attn_scr[at])
        attn_scr[pl.ds(rows + offset[2], count // 2, stride=stride)] = fold(out[2])
    attn_ref[...] = attn_scr[...].astype(bf16)


def product(first, half, attns, weights):
    total = None
    for attn, weight in zip(attns, weights):
        third = attn[2 * half :]
        if first:
            third = swap(third.astype(f32)).astype(bf16)
        rows = jnp.concatenate([attn[first : first + half], third[:, :HALF]], axis=1)
        part = jnp.dot(rows, weight[...], preferred_element_type=f32)
        total = part if total is None else total + part
    return total


def product_kernel(x_ref, *rest):
    out_ref, count = rest[-1], len(rest) // 2
    half = x_ref.shape[0] // 2
    for first in (0, half):
        at = slice(first, first + half)
        part = product(first, half, rest[:count], rest[count : 2 * count])
        out_ref[at] = x_ref[at].astype(f32) + part


def own_kernel(place, x_ref, attn_ref, w_ref, last_ref, out_ref, own_ref, last_own_ref):
    product_kernel(x_ref, attn_ref, w_ref, out_ref)
    cols = own_ref.shape[1]
    for i in range(out_ref.shape[1] // cols):

        @pl.when(place[0] == i)
        def _():
            at = slice(i * cols, (i + 1) * cols)
            own_ref[...] = out_ref[:, at]
            last_own_ref[...] = last_ref[:, at]


def output_kernel(x_ref, own_ref, last_own_ref, gb_ref, attn_ref, w_ref, out_hbm, out_ref, sems):
    copies = []
    rows, width = x_ref.shape
    step = rows // 4
    for i in range(4):
        at = slice(i * step, (i + 1) * step)
        third = attn_ref[rows + i % 2 * step : rows + (i % 2 + 1) * step]
        if i > 1:
            third = swap(third.astype(f32)).astype(bf16)
        attn = jnp.concatenate([attn_ref[at], third[:, :HALF]], axis=1)
        resid = x_ref[at] + jnp.dot(attn, w_ref[...], preferred_element_type=f32)
        mean = jnp.sum(resid, axis=1, keepdims=True) / width
        var = jnp.sum(resid * resid, axis=1, keepdims=True) / width - mean * mean
        mine = own_ref[at] + jnp.dot(attn, last_own_ref[...], preferred_element_type=f32)
        normed = (mine - mean) * lax.rsqrt(var + epsilon) * gb_ref[0:1] + gb_ref[1:2]
        out_ref[:, at] = normed.astype(bf16).T
        copies.append(pltpu.make_async_copy(out_ref.at[:, at], out_hbm.at[:, at], sems.at[i]))
        copies[i].start()
    for copy in copies:
        copy.wait()


IN_VMEM = pl.BlockSpec(memory_space=pltpu.VMEM)
IN_SMEM = pl.BlockSpec(memory_space=pltpu.SMEM)
IN_HBM = pl.BlockSpec(memory_space=pltpu.HBM)


def call(kernel, outs, scratch, scalars, far, near, name, flops, limit, held=None):
    return pl.pallas_call(
        kernel,
        out_shape=outs,
        in_specs=[IN_SMEM] * len(scalars) + [IN_HBM] * len(far) + [IN_VMEM] * len(near),
        out_specs=jax.tree.map(lambda _: held or IN_VMEM, outs),
        scratch_shapes=scratch,
        compiler_params=pltpu.CompilerParams(vmem_limit_bytes=limit << 20),
        name=name,
        cost_estimate=pl.CostEstimate(flops=flops, transcendentals=0, bytes_accessed=4 << 20),
    )(*scalars, *far, *near)


def local(tokens, w_qkv, w_out, gain, bias, mid_offset, far_offset):
    rows, width = tokens.shape
    heads_here = mid_offset.shape[0]
    head_size = width // HEADS
    cols = heads_here * head_size
    factor = math.log2(math.e) / math.sqrt(head_size)
    mid, far = rows // R1, rows // R2
    per = mid + far
    shape = jax.ShapeDtypeStruct
    after = lax.optimization_barrier

    head_count = lax.axis_size("head")
    if head_count & (head_count - 1) == 0:
        paths = [[(i, i ^ r) for i in range(head_count)] for r in range(head_count)]
    else:
        paths = [[(i, (i + r) % head_count) for i in range(head_count)] for r in range(head_count)]

    def to(array, r):
        return lax.ppermute(array, "head", paths[r])

    def spread(array):
        return [array] + [to(array, r) for r in range(1, head_count)]

    two_step = head_count == 4

    def pinned(array):
        return pltpu.with_memory_space_constraint(array, pltpu.HBM)

    x = pltpu.with_memory_space_constraint(tokens, pltpu.VMEM)
    w_rows = pltpu.with_memory_space_constraint(jnp.swapaxes(w_qkv, 1, 2), pltpu.VMEM)
    lanes = call(
        lanes_kernel, shape((8, LANES), jnp.int32), [], (), (), (), "lanes", 460 << 20, 24
    )
    offsets = (pinned(mid_offset), pinned(far_offset))
    told = [pltpu.SMEM((heads_here,), jnp.int32)] * 2
    kv, kvp = call(
        project_kernel,
        (
            shape((rows, 3 * LANES), bf16),
            shape((3 * per, LANES), bf16),
        ),
        [
            *told,
            pltpu.VMEM((3, rows, LANES), f32),
            pltpu.SemaphoreType.DMA((2,)),
        ],
        (),
        (),
        (mid_offset, far_offset, x, w_rows, lanes),
        "project",
        2 * rows * width * 2 * cols,
        24,
    )

    seq_count = lax.axis_size("seq")
    mid_devs = min(8, seq_count)

    def within(step):
        return [
            (i, i // mid_devs * mid_devs + (i + step) % mid_devs) for i in range(seq_count)
        ]

    if mid_devs == seq_count:
        mids = [kvp] + [lax.ppermute(kvp, "seq", within(s)) for s in range(1, mid_devs)]
        fars = None
    else:
        split = kvp.reshape(3, per, LANES)
        piece = split[:, :mid]
        mids = [piece] + [lax.ppermute(piece, "seq", within(s)) for s in range(1, mid_devs)]
        fars = [lax.all_gather(split[:, mid:], "seq", axis=1, tiled=True)]

    if two_step:
        across = to(after((w_out, lanes))[0], 2)
        beside = to(w_out, 1)
        weights = [w_out, beside, across, to(across, 1)]
    else:
        weights = spread(w_out)

    near, am, pk, qp, gb = call(
        partial(near_kernel, factor),
        (
            shape((rows + rows // 2, LANES), f32),
            shape((3 * per, LANES), f32),
            shape((3 * per, LANES), f32),
            shape((3 * per, LANES), bf16),
            shape((2, cols), f32),
        ),
        [
            *told,
            pltpu.VMEM((3, rows, LANES), f32),
            pltpu.VMEM((3, rows, LANES), f32),
            pltpu.VMEM((2, rows, LANES), f32),
            pltpu.VMEM((rows, 2 * LANES), bf16),
            pltpu.SemaphoreType.DMA((2,)),
        ],
        (),
        offsets,
        (kv, x, w_rows, gain.reshape(1, cols), bias.reshape(1, cols)),
        "near",
        1 << 29,
        24,
    )
    attn = call(
        partial(merge_kernel, factor, len(mids), len(fars or mids)),
        shape((rows + rows // 2, LANES), bf16),
        [
            *told,
            pltpu.VMEM((rows + rows // 2, LANES), f32),
            pltpu.VMEM((3, mid, LANES), f32),
            pltpu.VMEM((3, mid, LANES), f32),
            pltpu.SemaphoreType.DMA((2,)),
        ],
        (),
        (),
        (mid_offset, far_offset, near, qp, am, pk, *mids, *(fars or mids)),
        "merge",
        1 << 29,
        24,
    )
    if two_step:
        attn_across = to(attn, 2)
        attns = [attn, to(attn, 1), attn_across, to(attn_across, 1)]
    else:
        attns = spread(attn)

    flops = 2 * rows * cols * width
    resid = call(
        product_kernel,
        shape((rows, width), f32),
        [],
        (),
        (),
        (x, *attns[:-2], *weights[:-2]),
        "product",
        (head_count - 2) * flops,
        24,
    )
    resid, own, last_own = call(
        own_kernel,
        (
            shape((rows, width), f32),
            shape((rows, cols), f32),
            shape((cols, cols), bf16),
        ),
        [],
        (lax.axis_index("head").reshape(1),),
        (),
        (resid, attns[-2], *weights[-2:]),
        "own",
        flops,
        24,
    )
    out = call(
        output_kernel,
        shape((cols, rows), bf16),
        [pltpu.VMEM((cols, rows), bf16), pltpu.SemaphoreType.DMA((4,))],
        (),
        (),
        (resid, own, last_own, gb, attns[-1], weights[-1]),
        "output",
        flops,
        24,
        IN_HBM,
    )
    return out.T


def solution(mesh):
    in_specs = (
        P(("group", "seq"), None),
        P(None, None, "head"),
        P("head", None),
        P("head"),
        P("head"),
        P("head"),
        P("head"),
    )
    out_specs = P(("group", "seq"), "head")
    return jax.shard_map(local, mesh=mesh, in_specs=in_specs, out_specs=out_specs, check_vma=False)
```
